256 devices in a mesh: tensor: 8 (over z_hi, core), mirror: 2 (over z_lo), dp: 16 (over x, y).
Axes of the slice: x: 4, y: 4, z: 8 (z_hi: 4, z_lo: 2; z = z_hi * 2 + z_lo), core: 2. Of those that a mesh axis runs over, the one named last changes fastest.
Arguments:
- layer_input: bfloat16 [32, 256, 4096], P(('mirror', 'dp'), 'tensor'), may hold values from -6 to 6
- qk_weight: bfloat16 [4096, 2, 4096], P(None, None, 'tensor'), may hold values from -0.09375 to 0.09375
- query_proj: bfloat16 [32, 256, 4096], P(('mirror', 'dp'), None, 'tensor'), may hold values from -24 to 24
- key_proj: bfloat16 [32, 256, 4096], P(('mirror', 'dp'), None, 'tensor'), may hold values from -24 to 24
- value_proj: bfloat16 [32, 256, 4096], P(('mirror', 'dp'), None, 'tensor'), may hold values from -6 to 6
- head_grad: bfloat16 [32, 256, 4096], P(('mirror', 'dp'), None, 'tensor'), may hold values from -6 to 6
- doc_ids: int32 [32, 256], P(('mirror', 'dp')), may hold values from 0 to 3, as said below
Outputs:
- input_grad: bfloat16 [32, 256, 4096], P(('mirror', 'dp'), 'tensor')
- qk_weight_grad: float32 [4096, 2, 4096], P(('mirror', 'dp'), None, 'tensor')
The draws below stay inside these ranges and needn't reach their ends.
Inputs may be any that keep to these rules, and one draw needn't show every extreme that they name: `doc_ids`: within each sequence of 128 tokens the ids start at 0, never fall, and each of the four documents holds a multiple of 8 tokens.
All inputs are finite; a program needn't handle non-finite values.
Results may differ from the reference program's by a relative error of at most 0.023.
Values may be sent and summed in bfloat16 or wider, within the bound.
A program may use at most 128 MiB of HBM per device.

```python
import math
import jax
import jax.numpy as jnp
from jax import lax

D = 4096
HD = 128
SEQ = 128
MICRO = 2
TOK_DEV = 256
REPL = 32
N_TENSOR = 8


def document_ids(key_base):
    sequences = REPL * MICRO
    granule = SEQ // 16
    ranked = jax.random.randint(key_base, (sequences, 15), 0, 1 << 20) * 16 + jnp.arange(15)
    chosen = jnp.argsort(ranked, axis=1)[:, :3]
    cut_points = (chosen + 1) * granule
    positions = jnp.arange(SEQ)
    doc_index = jnp.sum((positions[None, :, None] >= cut_points[:, None, :]).astype(jnp.int32), axis=2)
    return doc_index.astype(jnp.int32).reshape(REPL, TOK_DEV)


def draw_doc_ids(key, part):
    return document_ids(jax.random.fold_in(key, 11))


def drawn_field(key, salt):
    base_field = jnp.clip(jax.random.normal(jax.random.fold_in(key, salt), (REPL, TOK_DEV, D), jnp.float32), -6.0, 6.0)
    return base_field


def draw_query_proj(key, part):
    return drawn_field(key, 21).astype(jnp.bfloat16)


def draw_key_proj(key, part):
    return drawn_field(key, 22).astype(jnp.bfloat16)


def strengthened(array, stream_key, source, target, blocks, factor):
    def block_of(position):
        return (jnp.arange(array.shape[position]) // (array.shape[position] // blocks)).reshape((-1,) + (1,) * (array.ndim - 1 - position))

    near = jax.random.permutation(stream_key, blocks)[block_of(target)]
    far = (block_of(target) + blocks // 2) % blocks
    return jnp.where((block_of(source) == near) | (block_of(source) == far), factor * array, array)


def levels(stream_key, dims, split, smallest, largest):
    level = 1.0
    for axis_at, parts in split:
        heights = jax.random.uniform(jax.random.fold_in(jax.random.fold_in(stream_key, 6), axis_at), (parts,), jnp.float32, smallest / len(split), largest / len(split))
        level = level * jnp.repeat(jnp.exp(heights), dims[axis_at] // parts).reshape((-1,) + (1,) * (len(dims) - 1 - axis_at))
    return level


def centred(rng, dims, spread, limit, cuts=(), kind=jnp.bfloat16):
    result = spread * jax.random.normal(rng, dims, jnp.float32)
    if cuts:
        result = result * levels(rng, dims, cuts, -0.22, 0.18)
    return jnp.clip(result, -limit, limit).astype(kind)


def gaussian_with(rng, dims, deviation, bound, pieces, heavy, held_as=jnp.bfloat16):
    entries = deviation * jax.random.normal(rng, dims, jnp.float32)
    if pieces:
        entries = entries * levels(rng, dims, pieces, -0.22, 0.18)
    return jnp.clip(strengthened(entries, jax.random.fold_in(rng, 3), *heavy), -bound, bound).astype(held_as)


def setup_inputs(seed: int = 0) -> dict:
    splits = jax.random.split(jax.random.key(seed), 8)
    layer_input = gaussian_with(splits[0], (REPL, TOK_DEV, D), 1.0, 6.0, ((0, 32), (1, 8)), (0, 2, 32, 2.75))
    qk_weight = centred(splits[1], (D, 2, D), D ** -0.5, 0.09375, ((2, 8),))
    query_proj = draw_query_proj(jax.random.fold_in(splits[7], 71), 0)
    key_proj = draw_key_proj(jax.random.fold_in(splits[7], 71), 0)
    value_proj = centred(splits[4], (REPL, TOK_DEV, D), 1.0, 6.0, ((0, 32), (2, 8)))
    head_grad = centred(splits[5], (REPL, TOK_DEV, D), 1.0, 6.0, ((0, 32), (2, 8)))
    doc_ids = draw_doc_ids(jax.random.fold_in(splits[7], 71), 0)
    return {"layer_input": layer_input, "qk_weight": qk_weight, "query_proj": query_proj, "key_proj": key_proj, "value_proj": value_proj, "head_grad": head_grad, "doc_ids": doc_ids}


def rotate_pairs(values, cosine, sine_table):
    half = values.shape[-1] // 2
    first_half = values[..., :half]
    second_half = values[..., half:]
    cos_b = cosine[None, :, None, :]
    sin_b = sine_table[None, :, None, :]
    return jnp.concatenate([first_half * cos_b - second_half * sin_b, second_half * cos_b + first_half * sin_b], axis=-1)

def unrotate_pairs(values, cosine, sine_table):
    half = values.shape[-1] // 2
    first_half = values[..., :half]
    second_half = values[..., half:]
    cos_b = cosine[None, :, None, :]
    sin_b = sine_table[None, :, None, :]
    return jnp.concatenate([first_half * cos_b + second_half * sin_b, second_half * cos_b - first_half * sin_b], axis=-1)

def attention_grads(query_rows, key_rows, value_rows, grad_rows, doc_row):
    token_count, full_width = query_rows.shape
    head_count = full_width // HD
    micro_count = token_count // SEQ
    shape_four = (micro_count, SEQ, head_count, HD)
    positions = jnp.arange(SEQ).astype(jnp.float32)
    inverse = jnp.exp(-(2.0 * jnp.arange(HD // 2).astype(jnp.float32) / HD) * math.log(10000.0))
    angles = positions[:, None] * inverse[None, :]
    cosine = jnp.cos(angles)
    sine_table = jnp.sin(angles)
    q_rot = rotate_pairs(query_rows.reshape(shape_four).astype(jnp.float32), cosine, sine_table).astype(jnp.bfloat16)
    k_rot = rotate_pairs(key_rows.reshape(shape_four).astype(jnp.float32), cosine, sine_table).astype(jnp.bfloat16)
    scale = 1.0 / math.sqrt(HD)
    scores = jnp.einsum('bshd,bthd->bhst', q_rot.astype(jnp.float32), k_rot.astype(jnp.float32)) * scale
    docs = doc_row.reshape(micro_count, SEQ)
    index_seq = jnp.arange(SEQ)
    causal = index_seq[None, :] <= index_seq[:, None]
    allowed = causal[None, :, :] & (docs[:, :, None] == docs[:, None, :])
    scores = jnp.where(allowed[:, None, :, :], scores, -1e+30)
    highest = lax.optimization_barrier(jnp.max(scores, axis=-1, keepdims=True))
    exps = jnp.exp(scores - highest)
    probs = exps / lax.optimization_barrier(jnp.sum(exps, axis=-1, keepdims=True))
    dprob = jnp.einsum('bshd,bthd->bhst', grad_rows.reshape(shape_four).astype(jnp.float32), value_rows.reshape(shape_four).astype(jnp.float32))
    delta = lax.optimization_barrier(jnp.sum(probs * dprob, axis=-1, keepdims=True))
    dscore = (probs * (dprob - delta)).astype(jnp.bfloat16)
    dq_rot = jnp.einsum('bhst,bthd->bshd', dscore.astype(jnp.float32), k_rot.astype(jnp.float32)) * scale
    dk_rot = jnp.einsum('bhst,bshd->bthd', dscore.astype(jnp.float32), q_rot.astype(jnp.float32)) * scale
    query_grad = unrotate_pairs(dq_rot, cosine, sine_table).astype(jnp.bfloat16).reshape(token_count, full_width)
    key_grad = unrotate_pairs(dk_rot, cosine, sine_table).astype(jnp.bfloat16).reshape(token_count, full_width)
    return (query_grad, key_grad)

def reference(layer_input, qk_weight, query_proj, key_proj, value_proj, head_grad, doc_ids):
    group_width = D // N_TENSOR
    weight_groups = qk_weight.astype(jnp.float32).reshape(D, 2, N_TENSOR, group_width)

    def replica_step(accumulated, slices_in):
        inputs_rows, query_rows, key_rows, value_rows, grad_rows, doc_row = slices_in
        query_grad, key_grad = attention_grads(query_rows, key_rows, value_rows, grad_rows, doc_row)
        stacked = jnp.stack([query_grad, key_grad], axis=1).astype(jnp.float32)
        partials = jnp.einsum('tjnc,djnc->ntd', stacked.reshape(TOK_DEV, 2, N_TENSOR, group_width), weight_groups)
        partials = lax.optimization_barrier(partials.astype(jnp.bfloat16)).astype(jnp.float32)
        input_rows = lax.optimization_barrier(jnp.sum(partials, axis=0)).astype(jnp.bfloat16)
        term = jnp.einsum('ti,tjc->ijc', inputs_rows.astype(jnp.float32), stacked)
        term = lax.optimization_barrier(term.astype(jnp.bfloat16)).astype(jnp.float32)
        return (accumulated + term, input_rows)
    start_sum = jnp.zeros((D, 2, D), jnp.float32)
    accumulated, input_grad = lax.scan(replica_step, start_sum, (layer_input, query_proj, key_proj, value_proj, head_grad, doc_ids))
    return (input_grad, accumulated / REPL)
```

```python
import functools
import math

import jax
import jax.numpy as jnp
import numpy as np
from jax import lax
from jax.experimental import pallas as pl
from jax.experimental.pallas import tpu as pltpu
from jax.sharding import PartitionSpec as P

HD = 128
SEQ = 128
MESH = pl.DeviceIdType.MESH
NT = (((1,), (1,)), ((), ()))
TN = (((0,), (0,)), ((), ()))
BF16 = jnp.bfloat16
F32 = jnp.float32
COPIES = 96


def rope_tables():
    positions = np.arange(SEQ).astype(np.float32)
    inverse = np.exp(
        -(np.float32(2.0) * np.arange(HD // 2).astype(np.float32) / np.float32(HD))
        * np.float32(math.log(10000.0))
    )
    angles = positions[:, None] * inverse[None, :].astype(np.float32)
    cosine = np.cos(angles).astype(np.float32)
    sine = np.sin(angles).astype(np.float32)
    return (
        np.concatenate([cosine, cosine], axis=1),
        np.concatenate([-sine, sine], axis=1),
    )


def kernel(
    x_ref, w_hbm, q_ref, k_ref, v_ref, g_ref, doc_ref, cos_ref, sin_ref,
    ig_ref, wg_ref,
    w_buf, x_buf, g_buf, g_tok, p_buf, p_sib, z_out, z_one, z_two,
    t_buf, r_one, r_two, m_out, m_in,
    w_sem, l_sem, send_sem, recv_sem,
):
    t = lax.axis_index("tensor")
    m = lax.axis_index("mirror")
    d = lax.axis_index("dp")
    zh, c = lax.div(t, 2), lax.rem(t, 2)
    x, y = lax.div(d, 4), lax.rem(d, 4)

    def at_z(step):
        return {"tensor": lax.rem(zh + step, 4) * 2 + c}

    def at_x(step):
        return {"dp": lax.rem(x + step, 4) * 4 + y}

    def at_y(step):
        return {"dp": x * 4 + lax.rem(y + step, 4)}

    sibling = {"tensor": zh * 2 + 1 - c}
    twin = {"mirror": 1 - m}

    w_in = [
        pltpu.make_async_copy(w_hbm.at[pl.ds(i * 512, 512)], w_buf.at[i], w_sem.at[i])
        for i in range(8)
    ]
    for copy in w_in:
        copy.start()
    halves = (1 - m, m)
    own_in = [
        pltpu.make_async_copy(
            x_ref.at[0, :, pl.ds(pl.multiple_of(halves[u] * 2048 + x * 512, 512), 512)],
            x_buf.at[u, 0, pl.ds(pl.multiple_of(t * 32, 32), 32)],
            l_sem.at[u],
        )
        for u in range(2)
    ]
    for copy in own_in:
        copy.start()

    barrier = pltpu.get_barrier_semaphore()
    partners = [sibling, at_z(1), at_z(3), at_x(1), at_x(2), at_x(3), at_y(1), at_y(3), twin]
    for partner in partners:
        pl.semaphore_signal(barrier, inc=1, device_id=partner, device_id_type=MESH)
    pl.semaphore_wait(barrier, len(partners))

    sent = []

    def send(src, dst, device):
        index = len(sent)
        copy = pltpu.make_async_remote_copy(
            src_ref=src,
            dst_ref=dst,
            send_sem=send_sem.at[index],
            recv_sem=recv_sem.at[index],
            device_id=device,
            device_id_type=MESH,
        )
        copy.start()
        sent.append(copy)
        return copy

    turned = []
    for u in range(2):
        for step in (1, 3, 2):
            column = pl.multiple_of(halves[u] * 2048 + lax.rem(x + step, 4) * 512, 512)
            turned.append(
                send(
                    x_ref.at[0, :, pl.ds(column, 512)],
                    x_buf.at[u, 4 - step, pl.ds(pl.multiple_of(t * 32, 32), 32)],
                    at_x(step),
                )
            )

    def piece(which, zi, half=None):
        start = (lax.rem(zi, 4) * 2 + c) * 32
        if half is None:
            rows = pl.ds(pl.multiple_of(start, 32), 32)
        else:
            rows = pl.ds(pl.multiple_of(start + 16 * half, 16), 16)
        if which == 0:
            return x_buf.at[:, 0, rows]
        return x_buf.at[which - 1, pl.ds(1, 3), rows]

    ring = {}

    def x_start(which):
        own = piece(which, zh)
        ring[which] = [send(own, own, at_z(1)), send(own, own, at_z(3))]
        ring[which, "sib"] = [send(own, own, sibling)]

    def x_forward(which):
        up, down = ring[which]
        up.wait_recv()
        half = piece(which, zh + 3, 0)
        fu = send(half, half, at_z(1))
        whole = piece(which, zh + 3)
        s_up = send(whole, whole, sibling)
        down.wait_recv()
        half = piece(which, zh + 1, 1)
        fd = send(half, half, at_z(3))
        whole = piece(which, zh + 1)
        s_down = send(whole, whole, sibling)
        ring[which, "far"] = [fu, fd]
        ring[which, "sib"] += [s_up, s_down]

    def x_far(which):
        fu, fd = ring[which, "far"]
        fu.wait_recv()
        half = piece(which, zh + 2, 0)
        s_up = send(half, half, sibling)
        fd.wait_recv()
        half = piece(which, zh + 2, 1)
        s_down = send(half, half, sibling)
        ring[which, "sib"] += [s_up, s_down]

    def x_finish(which):
        for copy in ring[which, "sib"]:
            copy.wait_recv()

    for copy in own_in:
        copy.wait()
    x_start(0)

    cosine, sine = cos_ref[...], sin_ref[...]
    scale = 1.0 / math.sqrt(HD)
    row = lax.broadcasted_iota(jnp.int32, (SEQ, SEQ), 0)
    col = lax.broadcasted_iota(jnp.int32, (SEQ, SEQ), 1)
    allowed = []
    for s in range(2):
        docs = jnp.broadcast_to(doc_ref[:, s * SEQ : (s + 1) * SEQ].astype(F32), (SEQ, SEQ))
        allowed.append((col <= row) & (docs == docs.T))

    def rotate(values):
        return values * cosine + pltpu.roll(values, 64, 1) * sine

    def unrotate(values):
        return values * cosine - pltpu.roll(values, 64, 1) * sine

    def heads(pair):
        for s in range(2):
            rows = slice(s * SEQ, (s + 1) * SEQ)
            for j in range(2):
                h = 2 * pair + j
                cols = slice(h * HD, (h + 1) * HD)
                q_rot = rotate(q_ref[0, rows, cols].astype(F32)).astype(BF16)
                k_rot = rotate(k_ref[0, rows, cols].astype(F32)).astype(BF16)
                scores = lax.dot_general(q_rot, k_rot, NT, preferred_element_type=F32) * scale
                scores = jnp.where(allowed[s], scores, -1e30)
                exps = jnp.exp(scores - jnp.max(scores, axis=-1, keepdims=True))
                probs = exps / jnp.sum(exps, axis=-1, keepdims=True)
                dprob = lax.dot_general(
                    g_ref[0, rows, cols], v_ref[0, rows, cols], NT, preferred_element_type=F32
                )
                delta = jnp.sum(probs * dprob, axis=-1, keepdims=True)
                dscore = (probs * (dprob - delta)).astype(BF16)
                dq = jnp.dot(dscore, k_rot, preferred_element_type=F32) * scale
                dk = lax.dot_general(dscore, q_rot, TN, preferred_element_type=F32) * scale
                dq, dk = unrotate(dq), unrotate(dk)
                g_tok[rows, h * HD : (h + 1) * HD] = dq.astype(BF16)
                g_tok[rows, 512 + h * HD : 512 + (h + 1) * HD] = dk.astype(BF16)
                g_buf[pair, j * 256 : j * 256 + 128, rows] = dq.T.astype(BF16)
                g_buf[pair, j * 256 + 128 : j * 256 + 256, rows] = dk.T.astype(BF16)

    grads = {}

    def g_slot(pair, slot):
        return g_buf.at[pair, :, pl.ds(slot * 256, 256)]

    def g_start(pair):
        grads[pair] = [
            send(g_slot(pair, 0), g_slot(pair, 3), at_x(1)),
            send(g_slot(pair, 0), g_slot(pair, 1), at_x(3)),
        ]

    def g_forward(pair):
        up, down = grads[pair]
        low, high = pl.ds(0, 256), pl.ds(256, 256)
        up.wait_recv()
        fu = send(
            g_buf.at[pair, low, pl.ds(768, 256)], g_buf.at[pair, low, pl.ds(512, 256)], at_x(1)
        )
        down.wait_recv()
        fd = send(
            g_buf.at[pair, high, pl.ds(256, 256)], g_buf.at[pair, high, pl.ds(512, 256)], at_x(3)
        )
        grads[pair, "far"] = [fu, fd]

    def g_finish(pair):
        for copy in grads[pair, "far"]:
            copy.wait_recv()

    pick_row = lax.broadcasted_iota(jnp.int32, (256, 256), 0)
    pick_col = lax.broadcasted_iota(jnp.int32, (256, 256), 1)
    pick = jnp.where(
        pick_col == jnp.where(pick_row < 128, 2 * pick_row, 2 * pick_row - 255), 1.0, 0.0
    ).astype(BF16)
    swaps = {}

    def p_unit(u):
        for i in (2 * u, 2 * u + 1):
            w_in[i].wait()
            mixed = w_buf[i].reshape(1024, 512)
            parts = [
                jnp.dot(pick, mixed[b * 256 : (b + 1) * 256], preferred_element_type=F32).astype(
                    BF16
                )
                for b in range(4)
            ]
            w_q = jnp.concatenate([part[:128] for part in parts], axis=0)
            w_k = jnp.concatenate([part[128:] for part in parts], axis=0)
            partial = lax.dot_general(
                g_tok[:, :512], w_q, NT, preferred_element_type=F32
            ) + lax.dot_general(g_tok[:, 512:], w_k, NT, preferred_element_type=F32)
            off = (i % 2) * 512
            p_buf[u, :, :, :, off : off + 512] = partial.astype(BF16).reshape(4, 2, 32, 512)
        swaps[u] = send(p_buf.at[u, :, 1 - c], p_sib.at[u], sibling)

    def p_sum(u, zi):
        return p_buf[u, zi, c].astype(F32) + p_sib[u, zi].astype(F32)

    def p_one(u):
        swaps[u].wait_recv()
        z_out[u, 0] = p_sum(u, lax.rem(zh + 2, 4)).astype(BF16)
        low, high = pl.ds(0, 16), pl.ds(16, 16)
        swaps[u, 1] = [
            send(z_out.at[u, 0, low], z_one.at[u, 0], at_z(1)),
            send(z_out.at[u, 0, high], z_one.at[u, 1], at_z(3)),
        ]

    def p_two(u):
        up, down = swaps[u, 1]
        up.wait_recv()
        total = p_sum(u, lax.rem(zh + 1, 4))
        z_out[u, 1, :16] = (total[:16] + z_one[u, 0].astype(F32)).astype(BF16)
        z_out[u, 1, 16:] = total[16:].astype(BF16)
        fu = send(z_out.at[u, 1], z_two.at[u, 0], at_z(1))
        down.wait_recv()
        total = p_sum(u, lax.rem(zh + 3, 4))
        z_out[u, 2, :16] = total[:16].astype(BF16)
        z_out[u, 2, 16:] = (total[16:] + z_one[u, 1].astype(F32)).astype(BF16)
        fd = send(z_out.at[u, 2], z_two.at[u, 1], at_z(3))
        swaps[u, 2] = [fu, fd]

    def p_end(u):
        for copy in swaps[u, 2]:
            copy.wait_recv()
        total = p_sum(u, zh) + z_two[u, 0].astype(F32) + z_two[u, 1].astype(F32)
        ig_ref[:, u * 1024 : (u + 1) * 1024] = total.astype(BF16)

    terms = {}

    def t_unit(u, pair):
        term = jnp.dot(g_buf[pair], x_buf[u].reshape(1024, 512), preferred_element_type=F32)
        for b in range(4):
            t_buf[u, pair, b] = term[:, b * 128 : (b + 1) * 128].astype(BF16)
        far = lax.rem(y + 2, 4)
        n = 2 * u + pair
        terms[n] = [
            send(t_buf.at[u, pair, far, pl.ds(0, 256)], r_one.at[n, 0], at_y(1)),
            send(t_buf.at[u, pair, far, pl.ds(256, 256)], r_one.at[n, 1], at_y(3)),
        ]

    def t_two(u, pair):
        n = 2 * u + pair
        up, down = terms[n]
        up.wait_recv()
        b = lax.rem(y + 1, 4)
        t_buf[u, pair, b, :256] = (
            t_buf[u, pair, b, :256].astype(F32) + r_one[n, 0].astype(F32)
        ).astype(BF16)
        fu = send(t_buf.at[u, pair, b], r_two.at[n, 0], at_y(1))
        down.wait_recv()
        b = lax.rem(y + 3, 4)
        t_buf[u, pair, b, 256:] = (
            t_buf[u, pair, b, 256:].astype(F32) + r_one[n, 1].astype(F32)
        ).astype(BF16)
        fd = send(t_buf.at[u, pair, b], r_two.at[n, 1], at_y(3))
        terms[n, 2] = [fu, fd]

    def t_sum(u, pair):
        n = 2 * u + pair
        for copy in terms[n, 2]:
            copy.wait_recv()
        return (
            t_buf[u, pair, y].astype(F32) + r_two[n, 0].astype(F32) + r_two[n, 1].astype(F32)
        )

    def t_away(pair):
        m_out[pair] = t_sum(0, pair).astype(BF16)
        terms["m", pair] = send(m_out.at[pair], m_in.at[pair], twin)

    def t_end(pair):
        total = t_sum(1, pair)
        terms["m", pair].wait_recv()
        total = (total + m_in[pair].astype(F32)) * (1.0 / 32.0)
        for j in range(2):
            for p in range(2):
                block = total[j * 256 + p * 128 : j * 256 + p * 128 + 128]
                at = p * 512 + (2 * pair + j) * 128
                wg_ref[:, at : at + 128] = block.T

    heads(0)
    g_start(0)
    for copy in turned:
        copy.wait_recv()
    x_start(1)
    x_start(2)
    heads(1)
    g_start(1)
    p_unit(0)
    x_forward(0)
    p_unit(1)
    p_unit(2)
    g_forward(0)
    x_forward(1)
    x_far(0)
    p_unit(3)
    x_forward(2)
    g_forward(1)
    x_far(1)
    x_finish(0)
    x_finish(1)
    g_finish(0)
    t_unit(0, 0)
    p_one(0)
    p_one(1)
    t_two(0, 0)
    g_finish(1)
    t_unit(0, 1)
    x_far(2)
    p_one(2)
    p_one(3)
    x_finish(2)
    t_unit(1, 0)
    t_unit(1, 1)
    p_two(0)
    t_two(0, 1)
    t_away(0)
    p_two(1)
    t_two(1, 0)
    t_away(1)
    p_two(2)
    t_two(1, 1)
    p_two(3)
    p_end(0)
    t_end(0)
    p_end(1)
    t_end(1)
    p_end(2)
    p_end(3)
    for copy in sent:
        copy.wait_send()


def shards(layer_input, qk_weight, query_proj, key_proj, value_proj, head_grad, doc_ids):
    cosine, sine = rope_tables()
    vmem = pl.BlockSpec(memory_space=pltpu.VMEM)
    dma = pltpu.SemaphoreType.DMA
    input_grad, weight_grad = pl.pallas_call(
        kernel,
        out_shape=(
            jax.ShapeDtypeStruct((32, 4096), BF16),
            jax.ShapeDtypeStruct((128, 1024), F32),
        ),
        in_specs=[vmem, pl.BlockSpec(memory_space=pl.ANY)] + [vmem] * 7,
        out_specs=(vmem, vmem),
        scratch_shapes=[
            pltpu.VMEM((8, 512, 2, 512), BF16),
            pltpu.VMEM((2, 4, 256, 512), BF16),
            pltpu.VMEM((2, 512, 1024), BF16),
            pltpu.VMEM((256, 1024), BF16),
            pltpu.VMEM((4, 4, 2, 32, 1024), BF16),
            pltpu.VMEM((4, 4, 32, 1024), BF16),
            pltpu.VMEM((4, 3, 32, 1024), BF16),
            pltpu.VMEM((4, 2, 16, 1024), BF16),
            pltpu.VMEM((4, 2, 32, 1024), BF16),
            pltpu.VMEM((2, 2, 4, 512, 128), BF16),
            pltpu.VMEM((4, 2, 256, 128), BF16),
            pltpu.VMEM((4, 2, 512, 128), BF16),
            pltpu.VMEM((2, 512, 128), BF16),
            pltpu.VMEM((2, 512, 128), BF16),
            dma((8,)),
            dma((2,)),
            dma((COPIES,)),
            dma((COPIES,)),
        ],
        compiler_params=pltpu.CompilerParams(
            collective_id=0, has_side_effects=True, vmem_limit_bytes=58 << 20
        ),
        name="qk_backward",
    )(
        layer_input, qk_weight, query_proj, key_proj, value_proj, head_grad, doc_ids,
        jnp.asarray(cosine), jnp.asarray(sine),
    )
    return (input_grad.reshape(1, 32, 4096), weight_grad.reshape(128, 2, 512))


def solution(mesh):
    rows = ("mirror", "dp")
    in_specs = (
        P(rows, "tensor", None),
        P(None, None, "tensor"),
        P(rows, None, "tensor"),
        P(rows, None, "tensor"),
        P(rows, None, "tensor"),
        P(rows, None, "tensor"),
        P(rows, None),
    )
    out_specs = (P(rows, "tensor", None), P(rows, None, "tensor"))
    return jax.shard_map(shards, mesh=mesh, in_specs=in_specs, out_specs=out_specs, check_vma=False)
```

```python
import functools
import math

import jax
import jax.numpy as jnp
import numpy as np
from jax import lax
from jax.experimental import pallas as pl
from jax.experimental.pallas import tpu as pltpu
from jax.sharding import PartitionSpec as P

HD = 128
SEQ = 128
MESH = pl.DeviceIdType.MESH
NT = (((1,), (1,)), ((), ()))
TN = (((0,), (0,)), ((), ()))
BF16 = jnp.bfloat16
F32 = jnp.float32
COPIES = 112
SLOT = {1: 1, 3: 2, 2: 3}


def rope_tables():
    positions = np.arange(SEQ).astype(np.float32)
    inverse = np.exp(
        -(np.float32(2.0) * np.arange(HD // 2).astype(np.float32) / np.float32(HD))
        * np.float32(math.log(10000.0))
    )
    angles = positions[:, None] * inverse[None, :].astype(np.float32)
    cosine = np.cos(angles).astype(np.float32)
    sine = np.sin(angles).astype(np.float32)
    return (
        np.concatenate([cosine, cosine], axis=1),
        np.concatenate([-sine, sine], axis=1),
    )


def kernel(
    x_hbm, w_hbm, q_hbm, k_hbm, v_hbm, g_hbm, doc_hbm, cos_hbm, sin_hbm,
    ig_hbm, wg_hbm,
    x_ref, keep_ref, q_ref, k_ref, v_ref, g_ref, doc_ref, cos_ref, sin_ref, ig_ref, wg_ref,
    w_buf, x_buf, g_buf, g_tok, p_buf, p_sib, z_out, z_one, z_two,
    t_buf, r_one, r_two, m_out, m_in,
    l_sem, send_sem, recv_sem,
):
    t = lax.axis_index("tensor")
    m = lax.axis_index("mirror")
    d = lax.axis_index("dp")
    zh, c = lax.div(t, 2), lax.rem(t, 2)
    x, y = lax.div(d, 4), lax.rem(d, 4)

    def at_z(step):
        return {"tensor": lax.rem(zh + step, 4) * 2 + c}

    def at_x(step):
        return {"dp": lax.rem(x + step, 4) * 4 + y}

    def at_y(step):
        return {"dp": x * 4 + lax.rem(y + step, 4)}

    sibling = {"tensor": zh * 2 + 1 - c}
    twin = {"mirror": 1 - m}

    barrier = pltpu.get_barrier_semaphore()
    partners = [sibling, at_z(1), at_z(3), at_x(1), at_x(2), at_x(3), at_y(1), at_y(3), twin]
    for partner in partners:
        pl.semaphore_signal(barrier, inc=1, device_id=partner, device_id_type=MESH)

    def load(src, dst, index):
        copy = pltpu.make_async_copy(src, dst, l_sem.at[index])
        copy.start()
        return copy

    ready = [
        load(q_hbm.at[0], q_ref, 0),
        load(k_hbm.at[0], k_ref, 1),
        load(cos_hbm, cos_ref, 2),
        load(sin_hbm, sin_ref, 3),
        load(g_hbm.at[0], g_ref, 4),
        load(v_hbm.at[0], v_ref, 5),
        load(doc_hbm, doc_ref, 6),
    ]
    x_in = load(x_hbm.at[0], x_ref, 25)
    halves = (1 - m, m)
    own_in = [
        load(
            x_hbm.at[0, :, pl.ds(pl.multiple_of(halves[u] * 2048 + x * 512, 512), 512)],
            x_buf.at[u, 0, pl.ds(pl.multiple_of(t * 32, 32), 32)],
            7 + u,
        )
        for u in range(2)
    ]
    w_in = [load(w_hbm.at[pl.ds(i * 512, 512)], w_buf.at[i], 9 + i) for i in range(8)]
    def load_finish():
        for copy in ready:
            copy.wait()
        row = lax.broadcasted_iota(jnp.int32, (SEQ, SEQ), 0)
        col = lax.broadcasted_iota(jnp.int32, (SEQ, SEQ), 1)
        for s in range(2):
            docs = jnp.broadcast_to(doc_ref[:, s * SEQ : (s + 1) * SEQ].astype(F32), (SEQ, SEQ))
            keep_ref[s] = jnp.where((col <= row) & (docs == docs.T), 1.0, 0.0)

    def meet():
        pl.semaphore_wait(barrier, len(partners))

    sent = []

    def send(src, dst, device):
        index = len(sent)
        copy = pltpu.make_async_remote_copy(
            src_ref=src,
            dst_ref=dst,
            send_sem=send_sem.at[index],
            recv_sem=recv_sem.at[index],
            device_id=device,
            device_id_type=MESH,
        )
        copy.start()
        sent.append(copy)
        return copy

    turned = {}

    def turn(u):
        turned[u] = []
        for step in (1, 3, 2):
            column = pl.multiple_of(halves[u] * 2048 + lax.rem(x + step, 4) * 512, 512)
            turned[u].append(
                send(
                    x_ref.at[:, pl.ds(column, 512)],
                    x_buf.at[u, SLOT[step], pl.ds(pl.multiple_of(t * 32, 32), 32)],
                    at_x(step),
                )
            )

    def turn_near(u):
        turned[u][0].wait_recv()
        turned[u][1].wait_recv()

    def turn_far(u):
        turned[u][2].wait_recv()

    def own_finish():
        x_in.wait()
        for copy in own_in:
            copy.wait()

    def piece(which, zi, half=None):
        start = (lax.rem(zi, 4) * 2 + c) * 32
        if half is None:
            rows = pl.ds(pl.multiple_of(start, 32), 32)
        else:
            rows = pl.ds(pl.multiple_of(start + 16 * half, 16), 16)
        return (
            x_buf.at[:, 0, rows],
            x_buf.at[0, pl.ds(1, 2), rows],
            x_buf.at[0, 3, rows],
            x_buf.at[1, pl.ds(1, 3), rows],
        )[which]

    ring = {}

    def x_start(which):
        own = piece(which, zh)
        ring[which] = [send(own, own, at_z(1)), send(own, own, at_z(3))]
        ring[which, "sib"] = [send(own, own, sibling)]

    def x_forward(which):
        up, down = ring[which]
        up.wait_recv()
        half = piece(which, zh + 3, 0)
        fu = send(half, half, at_z(1))
        whole = piece(which, zh + 3)
        s_up = send(whole, whole, sibling)
        down.wait_recv()
        half = piece(which, zh + 1, 1)
        fd = send(half, half, at_z(3))
        whole = piece(which, zh + 1)
        s_down = send(whole, whole, sibling)
        ring[which, "far"] = [fu, fd]
        ring[which, "sib"] += [s_up, s_down]

    def x_far(which):
        fu, fd = ring[which, "far"]
        fu.wait_recv()
        half = piece(which, zh + 2, 0)
        s_up = send(half, half, sibling)
        fd.wait_recv()
        half = piece(which, zh + 2, 1)
        s_down = send(half, half, sibling)
        ring[which, "sib"] += [s_up, s_down]

    def x_finish(which):
        for copy in ring[which, "sib"]:
            copy.wait_recv()

    scale = 1.0 / math.sqrt(HD)

    def rotate(values):
        return values * cos_ref[...] + pltpu.roll(values, 64, 1) * sin_ref[...]

    def unrotate(values):
        return values * cos_ref[...] - pltpu.roll(values, 64, 1) * sin_ref[...]

    def head(pair, j):
        h = 2 * pair + j
        for s in range(2):
            rows = slice(s * SEQ, (s + 1) * SEQ)
            cols = slice(h * HD, (h + 1) * HD)
            q_rot = rotate(q_ref[rows, cols].astype(F32)).astype(BF16)
            k_rot = rotate(k_ref[rows, cols].astype(F32)).astype(BF16)
            scores = lax.dot_general(q_rot, k_rot, NT, preferred_element_type=F32) * scale
            scores = jnp.where(keep_ref[s] > 0.5, scores, -1e30)
            exps = jnp.exp(scores - jnp.max(scores, axis=-1, keepdims=True))
            probs = exps / jnp.sum(exps, axis=-1, keepdims=True)
            dprob = lax.dot_general(
                g_ref[rows, cols], v_ref[rows, cols], NT, preferred_element_type=F32
            )
            delta = jnp.sum(probs * dprob, axis=-1, keepdims=True)
            dscore = (probs * (dprob - delta)).astype(BF16)
            dq = jnp.dot(dscore, k_rot, preferred_element_type=F32) * scale
            dk = lax.dot_general(dscore, q_rot, TN, preferred_element_type=F32) * scale
            dq, dk = unrotate(dq), unrotate(dk)
            g_tok[rows, h * HD : (h + 1) * HD] = dq.astype(BF16)
            g_tok[rows, 512 + h * HD : 512 + (h + 1) * HD] = dk.astype(BF16)
            g_buf[pair, j * 256 : j * 256 + 128, rows] = dq.T.astype(BF16)
            g_buf[pair, j * 256 + 128 : j * 256 + 256, rows] = dk.T.astype(BF16)

    grads = {}

    def g_part(h, slot, half=None):
        row, size = (h % 2) * 256, 256
        if half is not None:
            row, size = row + 128 * half, 128
        return g_buf.at[h // 2, pl.ds(row, size), pl.ds(slot * 256, 256)]

    def g_start(h):
        grads[h] = [
            send(g_part(h, 0), g_part(h, 1), at_x(1)),
            send(g_part(h, 0), g_part(h, 2), at_x(3)),
        ]

    def g_forward(h):
        up, down = grads[h]
        up.wait_recv()
        fu = send(g_part(h, 1, 0), g_part(h, 3, 0), at_x(1))
        down.wait_recv()
        fd = send(g_part(h, 2, 1), g_part(h, 3, 1), at_x(3))
        grads[h, "far"] = [fu, fd]

    def g_finish(pair):
        for h in (2 * pair, 2 * pair + 1):
            for copy in grads[h, "far"]:
                copy.wait_recv()

    pick_row = lax.broadcasted_iota(jnp.int32, (256, 256), 0)
    pick_col = lax.broadcasted_iota(jnp.int32, (256, 256), 1)
    pick = jnp.where(
        pick_col == jnp.where(pick_row < 128, 2 * pick_row, 2 * pick_row - 255), 1.0, 0.0
    ).astype(BF16)
    swaps = {}

    def p_unit(u):
        for i in (2 * u, 2 * u + 1):
            w_in[i].wait()
            mixed = w_buf[i].reshape(1024, 512)
            parts = [
                jnp.dot(pick, mixed[b * 256 : (b + 1) * 256], preferred_element_type=F32).astype(
                    BF16
                )
                for b in range(4)
            ]
            w_q = jnp.concatenate([part[:128] for part in parts], axis=0)
            w_k = jnp.concatenate([part[128:] for part in parts], axis=0)
            partial = lax.dot_general(
                g_tok[:, :512], w_q, NT, preferred_element_type=F32
            ) + lax.dot_general(g_tok[:, 512:], w_k, NT, preferred_element_type=F32)
            off = (i % 2) * 512
            p_buf[u, :, :, :, off : off + 512] = partial.astype(BF16).reshape(4, 2, 32, 512)
        swaps[u] = send(p_buf.at[u, :, 1 - c], p_sib.at[u], sibling)

    def p_sum(u, zi):
        return p_buf[u, zi, c].astype(F32) + p_sib[u, zi].astype(F32)

    def p_one(u):
        swaps[u].wait_recv()
        z_out[u, 0] = p_sum(u, lax.rem(zh + 2, 4)).astype(BF16)
        low, high = pl.ds(0, 16), pl.ds(16, 16)
        swaps[u, 1] = [
            send(z_out.at[u, 0, low], z_one.at[u, 0], at_z(1)),
            send(z_out.at[u, 0, high], z_one.at[u, 1], at_z(3)),
        ]

    def p_two(u):
        up, down = swaps[u, 1]
        up.wait_recv()
        total = p_sum(u, lax.rem(zh + 1, 4))
        z_out[u, 1, :16] = (total[:16] + z_one[u, 0].astype(F32)).astype(BF16)
        z_out[u, 1, 16:] = total[16:].astype(BF16)
        fu = send(z_out.at[u, 1], z_two.at[u, 0], at_z(1))
        down.wait_recv()
        total = p_sum(u, lax.rem(zh + 3, 4))
        z_out[u, 2, :16] = total[:16].astype(BF16)
        z_out[u, 2, 16:] = (total[16:] + z_one[u, 1].astype(F32)).astype(BF16)
        fd = send(z_out.at[u, 2], z_two.at[u, 1], at_z(3))
        swaps[u, 2] = [fu, fd]

    def p_end(u):
        for copy in swaps[u, 2]:
            copy.wait_recv()
        total = p_sum(u, zh) + z_two[u, 0].astype(F32) + z_two[u, 1].astype(F32)
        ig_ref[u] = total.astype(BF16)
        stored.append(load(ig_ref.at[u], ig_hbm.at[:, pl.ds(u * 1024, 1024)], 17 + u))

    terms = {}

    def t_unit(u, pair):
        term = jnp.dot(g_buf[pair], x_buf[u].reshape(1024, 512), preferred_element_type=F32)
        for b in range(4):
            t_buf[u, pair, b] = term[:, b * 128 : (b + 1) * 128].astype(BF16)
        far = lax.rem(y + 2, 4)
        n = 2 * u + pair
        terms[n] = [
            send(t_buf.at[u, pair, far, pl.ds(0, 256)], r_one.at[n, 0], at_y(1)),
            send(t_buf.at[u, pair, far, pl.ds(256, 256)], r_one.at[n, 1], at_y(3)),
        ]

    def t_two(u, pair):
        n = 2 * u + pair
        up, down = terms[n]
        up.wait_recv()
        b = lax.rem(y + 1, 4)
        t_buf[u, pair, b, :256] = (
            t_buf[u, pair, b, :256].astype(F32) + r_one[n, 0].astype(F32)
        ).astype(BF16)
        fu = send(t_buf.at[u, pair, b], r_two.at[n, 0], at_y(1))
        down.wait_recv()
        b = lax.rem(y + 3, 4)
        t_buf[u, pair, b, 256:] = (
            t_buf[u, pair, b, 256:].astype(F32) + r_one[n, 1].astype(F32)
        ).astype(BF16)
        fd = send(t_buf.at[u, pair, b], r_two.at[n, 1], at_y(3))
        terms[n, 2] = [fu, fd]

    def t_sum(u, pair):
        n = 2 * u + pair
        for copy in terms[n, 2]:
            copy.wait_recv()
        return (
            t_buf[u, pair, y].astype(F32) + r_two[n, 0].astype(F32) + r_two[n, 1].astype(F32)
        )

    def t_away(pair):
        m_out[pair] = t_sum(0, pair).astype(BF16)
        terms["m", pair] = send(m_out.at[pair], m_in.at[pair], twin)

    def t_end(pair):
        total = t_sum(1, pair)
        terms["m", pair].wait_recv()
        total = (total + m_in[pair].astype(F32)) * (1.0 / 32.0)
        for j in range(2):
            for p in range(2):
                block = total[j * 256 + p * 128 : j * 256 + p * 128 + 128]
                at = (2 * pair + j) * 128
                wg_ref[:, p, at : at + 128] = block.T
        span = pl.ds(pair * 256, 256)
        stored.append(load(wg_ref.at[:, :, span], wg_hbm.at[:, :, span], 21 + pair))

    stored = []

    load_finish()
    head(0, 0)
    own_finish()
    meet()
    turn(0)
    turn(1)
    x_start(0)
    g_start(0)
    head(0, 1)
    g_start(1)
    head(1, 0)
    head(1, 1)
    turn_near(0)
    x_start(1)
    turn_far(0)
    x_start(2)
    x_forward(0)
    p_unit(0)
    p_unit(1)
    x_forward(1)
    g_forward(0)
    p_unit(2)
    x_forward(2)
    turn_near(1)
    turn_far(1)
    x_start(3)
    p_one(0)
    p_one(1)
    g_forward(1)
    g_start(2)
    g_start(3)
    p_unit(3)
    x_far(0)
    x_far(1)
    x_far(2)
    x_finish(0)
    x_finish(1)
    x_finish(2)
    g_finish(0)
    t_unit(0, 0)
    g_forward(2)
    x_forward(3)
    p_one(2)
    p_one(3)
    t_two(0, 0)
    p_two(0)
    g_forward(3)
    p_two(1)
    x_far(3)
    g_finish(1)
    t_unit(0, 1)
    x_finish(3)
    t_unit(1, 0)
    t_unit(1, 1)
    t_away(0)
    p_two(2)
    p_two(3)
    t_two(0, 1)
    t_two(1, 0)
    t_two(1, 1)
    t_away(1)
    p_end(0)
    p_end(1)
    t_end(0)
    p_end(2)
    t_end(1)
    p_end(3)
    for copy in stored:
        copy.wait()
    for copy in sent:
        copy.wait_send()


def hand_over(ig_in, wg_in, ig_out, wg_out, ig_v, wg_v, sem):
    pairs = [(wg_in.at[pl.ds(64 * i, 64)], wg_v.at[pl.ds(64 * i, 64)]) for i in range(2)]
    pairs.append((ig_in, ig_v))
    outs = [wg_out.at[pl.ds(64 * i, 64)] for i in range(2)] + [ig_out.at[0]]
    loads = [pltpu.make_async_copy(a, b, sem.at[0, i]) for i, (a, b) in enumerate(pairs)]
    stores = [
        pltpu.make_async_copy(pairs[i][1], out, sem.at[1, i]) for i, out in enumerate(outs)
    ]
    for copy in loads:
        copy.start()
    for i in range(3):
        loads[i].wait()
        stores[i].start()
    for copy in stores:
        copy.wait()


def shards(layer_input, qk_weight, query_proj, key_proj, value_proj, head_grad, doc_ids):
    cosine, sine = rope_tables()
    hbm = pl.BlockSpec(memory_space=pl.ANY)
    dma = pltpu.SemaphoreType.DMA
    input_grad, weight_grad = pl.pallas_call(
        kernel,
        out_shape=(
            jax.ShapeDtypeStruct((32, 4096), BF16),
            jax.ShapeDtypeStruct((128, 2, 512), F32),
        ),
        in_specs=[hbm] * 9,
        out_specs=(hbm, hbm),
        scratch_shapes=[
            pltpu.VMEM((32, 4096), BF16),
            pltpu.VMEM((2, 128, 128), F32),
            pltpu.VMEM((256, 512), BF16),
            pltpu.VMEM((256, 512), BF16),
            pltpu.VMEM((256, 512), BF16),
            pltpu.VMEM((256, 512), BF16),
            pltpu.VMEM((1, 256), jnp.int32),
            pltpu.VMEM((128, 128), F32),
            pltpu.VMEM((128, 128), F32),
            pltpu.VMEM((4, 32, 1024), BF16),
            pltpu.VMEM((128, 2, 512), F32),
            pltpu.VMEM((8, 512, 2, 512), BF16),
            pltpu.VMEM((2, 4, 256, 512), BF16),
            pltpu.VMEM((2, 512, 1024), BF16),
            pltpu.VMEM((256, 1024), BF16),
            pltpu.VMEM((4, 4, 2, 32, 1024), BF16),
            pltpu.VMEM((4, 4, 32, 1024), BF16),
            pltpu.VMEM((4, 3, 32, 1024), BF16),
            pltpu.VMEM((4, 2, 16, 1024), BF16),
            pltpu.VMEM((4, 2, 32, 1024), BF16),
            pltpu.VMEM((2, 2, 4, 512, 128), BF16),
            pltpu.VMEM((4, 2, 256, 128), BF16),
            pltpu.VMEM((4, 2, 512, 128), BF16),
            pltpu.VMEM((2, 512, 128), BF16),
            pltpu.VMEM((2, 512, 128), BF16),
            dma((26,)),
            dma((COPIES,)),
            dma((COPIES,)),
        ],
        compiler_params=pltpu.CompilerParams(
            collective_id=0, has_side_effects=True, vmem_limit_bytes=58 << 20
        ),
        name="qk_backward",
    )(
        layer_input, qk_weight, query_proj, key_proj, value_proj, head_grad, doc_ids,
        jnp.asarray(cosine), jnp.asarray(sine),
    )
    return pl.pallas_call(
        hand_over,
        out_shape=(
            jax.ShapeDtypeStruct((1, 32, 4096), BF16),
            jax.ShapeDtypeStruct((128, 2, 512), F32),
        ),
        in_specs=[hbm] * 2,
        out_specs=(hbm, hbm),
        scratch_shapes=[
            pltpu.VMEM((32, 4096), BF16),
            pltpu.VMEM((128, 2, 512), F32),
            dma((2, 4)),
        ],
        compiler_params=pltpu.CompilerParams(vmem_limit_bytes=58 << 20),
        name="hand_over",
    )(input_grad, weight_grad)


def solution(mesh):
    rows = ("mirror", "dp")
    in_specs = (
        P(rows, "tensor", None),
        P(None, None, "tensor"),
        P(rows, None, "tensor"),
        P(rows, None, "tensor"),
        P(rows, None, "tensor"),
        P(rows, None, "tensor"),
        P(rows, None),
    )
    out_specs = (P(rows, "tensor", None), P(rows, None, "tensor"))
    return jax.shard_map(shards, mesh=mesh, in_specs=in_specs, out_specs=out_specs, check_vma=False)
```

```python
import functools
import math

import jax
import jax.numpy as jnp
import numpy as np
from jax import lax
from jax.experimental import pallas as pl
from jax.experimental.pallas import tpu as pltpu
from jax.sharding import PartitionSpec as P

HD = 128
SEQ = 128
MESH = pl.DeviceIdType.MESH
NT = (((1,), (1,)), ((), ()))
TN = (((0,), (0,)), ((), ()))
BF16 = jnp.bfloat16
F32 = jnp.float32
COPIES = 112
SLOT = {1: 1, 3: 2, 2: 3}


def rope_tables():
    positions = np.arange(SEQ).astype(np.float32)
    inverse = np.exp(
        -(np.float32(2.0) * np.arange(HD // 2).astype(np.float32) / np.float32(HD))
        * np.float32(math.log(10000.0))
    )
    angles = positions[:, None] * inverse[None, :].astype(np.float32)
    cosine = np.cos(angles).astype(np.float32)
    sine = np.sin(angles).astype(np.float32)
    return (
        np.concatenate([cosine, cosine], axis=1),
        np.concatenate([-sine, sine], axis=1),
    )


def kernel(
    x_hbm, w_hbm, q_hbm, k_hbm, v_hbm, g_hbm, doc_hbm, cos_hbm, sin_hbm,
    ig_ref, wg_ref,
    keep_ref, q_ref, k_ref, v_ref, g_ref, doc_ref, cos_ref, sin_ref,
    w_buf, x_buf, g_buf, g_tok, p_buf, p_sib, z_out, z_one, z_two,
    t_buf, r_one, r_two, m_out, m_in,
    l_sem, send_sem, recv_sem,
):
    t = lax.axis_index("tensor")
    m = lax.axis_index("mirror")
    d = lax.axis_index("dp")
    zh, c = lax.div(t, 2), lax.rem(t, 2)
    x, y = lax.div(d, 4), lax.rem(d, 4)

    def at_z(step):
        return {"tensor": lax.rem(zh + step, 4) * 2 + c}

    def at_x(step):
        return {"dp": lax.rem(x + step, 4) * 4 + y}

    def at_y(step):
        return {"dp": x * 4 + lax.rem(y + step, 4)}

    sibling = {"tensor": zh * 2 + 1 - c}
    twin = {"mirror": 1 - m}

    barrier = pltpu.get_barrier_semaphore()
    partners = [sibling, at_z(1), at_z(3), at_x(1), at_x(2), at_x(3), at_y(1), at_y(3), twin]
    for partner in partners:
        pl.semaphore_signal(barrier, inc=1, device_id=partner, device_id_type=MESH)

    def load(src, dst, index):
        copy = pltpu.make_async_copy(src, dst, l_sem.at[index])
        copy.start()
        return copy

    ready = [
        load(q_hbm.at[0], q_ref, 0),
        load(k_hbm.at[0], k_ref, 1),
        load(cos_hbm, cos_ref, 2),
        load(sin_hbm, sin_ref, 3),
        load(g_hbm.at[0], g_ref, 4),
        load(v_hbm.at[0], v_ref, 5),
        load(doc_hbm, doc_ref, 6),
    ]
    halves = (1 - m, m)
    own_in = [
        load(
            x_hbm.at[0, :, pl.ds(pl.multiple_of(halves[u] * 2048 + x * 512, 512), 512)],
            x_buf.at[u, 0, pl.ds(pl.multiple_of(t * 32, 32), 32)],
            7 + u,
        )
        for u in range(2)
    ]
    w_in = [load(w_hbm.at[pl.ds(i * 512, 512)], w_buf.at[i], 9 + i) for i in range(8)]
    def load_finish():
        for copy in ready:
            copy.wait()
        row = lax.broadcasted_iota(jnp.int32, (SEQ, SEQ), 0)
        col = lax.broadcasted_iota(jnp.int32, (SEQ, SEQ), 1)
        for s in range(2):
            docs = jnp.broadcast_to(doc_ref[:, s * SEQ : (s + 1) * SEQ].astype(F32), (SEQ, SEQ))
            keep_ref[s] = jnp.where((col <= row) & (docs == docs.T), 1.0, 0.0)

    def meet():
        pl.semaphore_wait(barrier, len(partners))

    sent = []

    def send(src, dst, device):
        index = len(sent)
        copy = pltpu.make_async_remote_copy(
            src_ref=src,
            dst_ref=dst,
            send_sem=send_sem.at[index],
            recv_sem=recv_sem.at[index],
            device_id=device,
            device_id_type=MESH,
        )
        copy.start()
        sent.append(copy)
        return copy

    turned = {}

    def turn(u):
        turned[u] = []
        for step in (1, 3, 2):
            column = pl.multiple_of(halves[u] * 2048 + lax.rem(x + step, 4) * 512, 512)
            turned[u].append(
                send(
                    x_hbm.at[0, :, pl.ds(column, 512)],
                    x_buf.at[u, SLOT[step], pl.ds(pl.multiple_of(t * 32, 32), 32)],
                    at_x(step),
                )
            )

    def turn_near(u):
        turned[u][0].wait_recv()
        turned[u][1].wait_recv()

    def turn_far(u):
        turned[u][2].wait_recv()

    def own_finish():
        for copy in own_in:
            copy.wait()

    def piece(which, zi, half=None):
        start = (lax.rem(zi, 4) * 2 + c) * 32
        if half is None:
            rows = pl.ds(pl.multiple_of(start, 32), 32)
        else:
            rows = pl.ds(pl.multiple_of(start + 16 * half, 16), 16)
        return (
            x_buf.at[:, 0, rows],
            x_buf.at[0, pl.ds(1, 2), rows],
            x_buf.at[0, 3, rows],
            x_buf.at[1, pl.ds(1, 3), rows],
        )[which]

    ring = {}

    def x_start(which):
        own = piece(which, zh)
        ring[which] = [send(own, own, at_z(1)), send(own, own, at_z(3))]
        ring[which, "sib"] = [send(own, own, sibling)]

    def x_forward(which):
        up, down = ring[which]
        up.wait_recv()
        half = piece(which, zh + 3, 0)
        fu = send(half, half, at_z(1))
        whole = piece(which, zh + 3)
        s_up = send(whole, whole, sibling)
        down.wait_recv()
        half = piece(which, zh + 1, 1)
        fd = send(half, half, at_z(3))
        whole = piece(which, zh + 1)
        s_down = send(whole, whole, sibling)
        ring[which, "far"] = [fu, fd]
        ring[which, "sib"] += [s_up, s_down]

    def x_far(which):
        fu, fd = ring[which, "far"]
        fu.wait_recv()
        half = piece(which, zh + 2, 0)
        s_up = send(half, half, sibling)
        fd.wait_recv()
        half = piece(which, zh + 2, 1)
        s_down = send(half, half, sibling)
        ring[which, "sib"] += [s_up, s_down]

    def x_finish(which):
        for copy in ring[which, "sib"]:
            copy.wait_recv()

    scale = 1.0 / math.sqrt(HD)

    def rotate(values):
        return values * cos_ref[...] + pltpu.roll(values, 64, 1) * sin_ref[...]

    def unrotate(values):
        return values * cos_ref[...] - pltpu.roll(values, 64, 1) * sin_ref[...]

    def head(pair, j):
        h = 2 * pair + j
        for s in range(2):
            rows = slice(s * SEQ, (s + 1) * SEQ)
            cols = slice(h * HD, (h + 1) * HD)
            q_rot = rotate(q_ref[rows, cols].astype(F32)).astype(BF16)
            k_rot = rotate(k_ref[rows, cols].astype(F32)).astype(BF16)
            scores = lax.dot_general(q_rot, k_rot, NT, preferred_element_type=F32) * scale
            scores = jnp.where(keep_ref[s] > 0.5, scores, -1e30)
            exps = jnp.exp(scores - jnp.max(scores, axis=-1, keepdims=True))
            probs = exps / jnp.sum(exps, axis=-1, keepdims=True)
            dprob = lax.dot_general(
                g_ref[rows, cols], v_ref[rows, cols], NT, preferred_element_type=F32
            )
            delta = jnp.sum(probs * dprob, axis=-1, keepdims=True)
            dscore = (probs * (dprob - delta)).astype(BF16)
            dq = jnp.dot(dscore, k_rot, preferred_element_type=F32) * scale
            dk = lax.dot_general(dscore, q_rot, TN, preferred_element_type=F32) * scale
            dq, dk = unrotate(dq), unrotate(dk)
            g_tok[rows, h * HD : (h + 1) * HD] = dq.astype(BF16)
            g_tok[rows, 512 + h * HD : 512 + (h + 1) * HD] = dk.astype(BF16)
            g_buf[pair, j * 256 : j * 256 + 128, rows] = dq.T.astype(BF16)
            g_buf[pair, j * 256 + 128 : j * 256 + 256, rows] = dk.T.astype(BF16)

    grads = {}

    def g_part(h, slot, half=0):
        first, size = ((0, 256), (0, 96), (96, 160))[half]
        row = (h % 2) * 256 + first
        return g_buf.at[h // 2, pl.ds(row, size), pl.ds(slot * 256, 256)]

    def g_start(h):
        grads[h] = [
            send(g_part(h, 0), g_part(h, 1), at_x(1)),
            send(g_part(h, 0), g_part(h, 2), at_x(3)),
        ]

    def g_forward(h):
        up, down = grads[h]
        up.wait_recv()
        fu = send(g_part(h, 1, 1), g_part(h, 3, 1), at_x(1))
        down.wait_recv()
        fd = send(g_part(h, 2, 2), g_part(h, 3, 2), at_x(3))
        grads[h, "far"] = [fu, fd]

    def g_finish(pair):
        for h in (2 * pair, 2 * pair + 1):
            for copy in grads[h, "far"]:
                copy.wait_recv()

    pick_row = lax.broadcasted_iota(jnp.int32, (256, 256), 0)
    pick_col = lax.broadcasted_iota(jnp.int32, (256, 256), 1)
    pick = jnp.where(
        pick_col == jnp.where(pick_row < 128, 2 * pick_row, 2 * pick_row - 255), 1.0, 0.0
    ).astype(BF16)
    swaps = {}

    def p_half(i):
        u, off = i // 2, (i % 2) * 512
        w_in[i].wait()
        mixed = w_buf[i].reshape(1024, 512)
        parts = [
            jnp.dot(pick, mixed[b * 256 : (b + 1) * 256], preferred_element_type=F32).astype(BF16)
            for b in range(4)
        ]
        w_q = jnp.concatenate([part[:128] for part in parts], axis=0)
        w_k = jnp.concatenate([part[128:] for part in parts], axis=0)
        partial = lax.dot_general(
            g_tok[:, :512], w_q, NT, preferred_element_type=F32
        ) + lax.dot_general(g_tok[:, 512:], w_k, NT, preferred_element_type=F32)
        p_buf[u, :, :, :, off : off + 512] = partial.astype(BF16).reshape(4, 2, 32, 512)
        if i % 2:
            swaps[u] = send(p_buf.at[u, :, 1 - c], p_sib.at[u], sibling)

    def p_sum(u, zi):
        return p_buf[u, zi, c].astype(F32) + p_sib[u, zi].astype(F32)

    def p_one(u):
        swaps[u].wait_recv()
        z_out[u, 0] = p_sum(u, lax.rem(zh + 2, 4)).astype(BF16)
        low, high = pl.ds(0, 16), pl.ds(16, 16)
        swaps[u, 1] = [
            send(z_out.at[u, 0, low], z_one.at[u, 0], at_z(1)),
            send(z_out.at[u, 0, high], z_one.at[u, 1], at_z(3)),
        ]

    def p_two(u):
        up, down = swaps[u, 1]
        up.wait_recv()
        total = p_sum(u, lax.rem(zh + 1, 4))
        z_out[u, 1, :16] = (total[:16] + z_one[u, 0].astype(F32)).astype(BF16)
        z_out[u, 1, 16:] = total[16:].astype(BF16)
        fu = send(z_out.at[u, 1], z_two.at[u, 0], at_z(1))
        down.wait_recv()
        total = p_sum(u, lax.rem(zh + 3, 4))
        z_out[u, 2, :16] = total[:16].astype(BF16)
        z_out[u, 2, 16:] = (total[16:] + z_one[u, 1].astype(F32)).astype(BF16)
        fd = send(z_out.at[u, 2], z_two.at[u, 1], at_z(3))
        swaps[u, 2] = [fu, fd]

    def p_end(u):
        for copy in swaps[u, 2]:
            copy.wait_recv()
        total = p_sum(u, zh) + z_two[u, 0].astype(F32) + z_two[u, 1].astype(F32)
        ig_ref[:, u * 1024 : (u + 1) * 1024] = total.astype(BF16)

    terms = {}

    def t_unit(u, pair):
        term = jnp.dot(g_buf[pair], x_buf[u].reshape(1024, 512), preferred_element_type=F32)
        for b in range(4):
            t_buf[u, pair, b] = term[:, b * 128 : (b + 1) * 128].astype(BF16)
        far = lax.rem(y + 2, 4)
        n = 2 * u + pair
        terms[n] = [
            send(t_buf.at[u, pair, far, pl.ds(0, 256)], r_one.at[n, 0], at_y(1)),
            send(t_buf.at[u, pair, far, pl.ds(256, 256)], r_one.at[n, 1], at_y(3)),
        ]

    def t_two(u, pair):
        n = 2 * u + pair
        up, down = terms[n]
        up.wait_recv()
        b = lax.rem(y + 1, 4)
        t_buf[u, pair, b, :256] = (
            t_buf[u, pair, b, :256].astype(F32) + r_one[n, 0].astype(F32)
        ).astype(BF16)
        fu = send(t_buf.at[u, pair, b], r_two.at[n, 0], at_y(1))
        down.wait_recv()
        b = lax.rem(y + 3, 4)
        t_buf[u, pair, b, 256:] = (
            t_buf[u, pair, b, 256:].astype(F32) + r_one[n, 1].astype(F32)
        ).astype(BF16)
        fd = send(t_buf.at[u, pair, b], r_two.at[n, 1], at_y(3))
        terms[n, 2] = [fu, fd]

    def t_sum(u, pair):
        n = 2 * u + pair
        for copy in terms[n, 2]:
            copy.wait_recv()
        return (
            t_buf[u, pair, y].astype(F32) + r_two[n, 0].astype(F32) + r_two[n, 1].astype(F32)
        )

    def t_away(pair):
        m_out[pair] = t_sum(0, pair).astype(BF16)
        terms["m", pair] = send(m_out.at[pair], m_in.at[pair], twin)

    def t_end(pair):
        total = t_sum(1, pair)
        terms["m", pair].wait_recv()
        total = (total + m_in[pair].astype(F32)) * (1.0 / 32.0)
        for j in range(2):
            for p in range(2):
                block = total[j * 256 + p * 128 : j * 256 + p * 128 + 128]
                at = (2 * pair + j) * 128
                wg_ref[:, p, at : at + 128] = block.T

    load_finish()
    head(0, 0)
    own_finish()
    meet()
    turn(0)
    x_start(0)
    turn(1)
    head(0, 1)
    head(1, 0)
    g_start(2)
    turn_near(0)
    x_start(1)
    g_start(0)
    head(1, 1)
    p_half(0)
    g_start(3)
    turn_far(0)
    x_start(2)
    p_half(1)
    x_forward(0)
    turn_near(1)
    p_half(2)
    p_half(3)
    turn_far(1)
    x_start(3)
    p_half(4)
    g_start(1)
    p_half(5)
    p_half(6)
    g_forward(2)
    x_far(0)
    x_forward(2)
    x_forward(1)
    p_one(2)
    x_finish(0)
    p_one(1)
    p_half(7)
    g_forward(3)
    p_one(3)
    g_forward(0)
    x_far(2)
    x_forward(3)
    g_forward(1)
    x_far(1)
    p_two(2)
    x_finish(1)
    g_finish(1)
    p_one(0)
    x_finish(2)
    t_unit(0, 1)
    g_finish(0)
    t_unit(0, 0)
    x_far(3)
    p_two(1)
    t_two(0, 1)
    p_two(3)
    x_finish(3)
    t_unit(1, 1)
    t_unit(1, 0)
    t_two(0, 0)
    p_end(2)
    p_two(0)
    t_away(1)
    t_two(1, 1)
    p_end(1)
    t_two(1, 0)
    t_away(0)
    p_end(3)
    p_end(0)
    t_end(1)
    t_end(0)
    for copy in sent:
        copy.wait_send()


def hand_over(ig_in, wg_in, ig_out, wg_out, sem):
    copies = [
        pltpu.make_async_copy(wg_in, wg_out, sem.at[0]),
        pltpu.make_async_copy(ig_in, ig_out.at[0], sem.at[1]),
    ]
    for copy in copies:
        copy.start()
    for copy in copies:
        copy.wait()


def shards(layer_input, qk_weight, query_proj, key_proj, value_proj, head_grad, doc_ids):
    cosine, sine = rope_tables()
    hbm = pl.BlockSpec(memory_space=pl.ANY)
    vmem = pl.BlockSpec(memory_space=pltpu.VMEM)
    dma = pltpu.SemaphoreType.DMA
    input_grad, weight_grad = pl.pallas_call(
        kernel,
        out_shape=(
            pltpu.VMEM((32, 4096), BF16),
            pltpu.VMEM((128, 2, 512), F32),
        ),
        in_specs=[hbm] * 9,
        out_specs=(vmem, vmem),
        scratch_shapes=[
            pltpu.VMEM((2, 128, 128), F32),
            pltpu.VMEM((256, 512), BF16),
            pltpu.VMEM((256, 512), BF16),
            pltpu.VMEM((256, 512), BF16),
            pltpu.VMEM((256, 512), BF16),
            pltpu.VMEM((1, 256), jnp.int32),
            pltpu.VMEM((128, 128), F32),
            pltpu.VMEM((128, 128), F32),
            pltpu.VMEM((8, 512, 2, 512), BF16),
            pltpu.VMEM((2, 4, 256, 512), BF16),
            pltpu.VMEM((2, 512, 1024), BF16),
            pltpu.VMEM((256, 1024), BF16),
            pltpu.VMEM((4, 4, 2, 32, 1024), BF16),
            pltpu.VMEM((4, 4, 32, 1024), BF16),
            pltpu.VMEM((4, 3, 32, 1024), BF16),
            pltpu.VMEM((4, 2, 16, 1024), BF16),
            pltpu.VMEM((4, 2, 32, 1024), BF16),
            pltpu.VMEM((2, 2, 4, 512, 128), BF16),
            pltpu.VMEM((4, 2, 256, 128), BF16),
            pltpu.VMEM((4, 2, 512, 128), BF16),
            pltpu.VMEM((2, 512, 128), BF16),
            pltpu.VMEM((2, 512, 128), BF16),
            dma((17,)),
            dma((COPIES,)),
            dma((COPIES,)),
        ],
        compiler_params=pltpu.CompilerParams(
            collective_id=0, has_side_effects=True, vmem_limit_bytes=58 << 20
        ),
        name="qk_backward",
    )(
        layer_input, qk_weight, query_proj, key_proj, value_proj, head_grad, doc_ids,
        jnp.asarray(cosine), jnp.asarray(sine),
    )
    return pl.pallas_call(
        hand_over,
        out_shape=(
            jax.ShapeDtypeStruct((1, 32, 4096), BF16),
            jax.ShapeDtypeStruct((128, 2, 512), F32),
        ),
        in_specs=[vmem] * 2,
        out_specs=(hbm, hbm),
        scratch_shapes=[dma((2,))],
        compiler_params=pltpu.CompilerParams(vmem_limit_bytes=16 << 20),
        name="hand_over",
    )(input_grad, weight_grad)


def solution(mesh):
    rows = ("mirror", "dp")
    in_specs = (
        P(rows, "tensor", None),
        P(None, None, "tensor"),
        P(rows, None, "tensor"),
        P(rows, None, "tensor"),
        P(rows, None, "tensor"),
        P(rows, None, "tensor"),
        P(rows, None),
    )
    out_specs = (P(rows, "tensor", None), P(rows, None, "tensor"))
    return jax.shard_map(shards, mesh=mesh, in_specs=in_specs, out_specs=out_specs, check_vma=False)
```

```python
import functools
import math

import jax
import jax.numpy as jnp
import numpy as np
from jax import lax
from jax.experimental import pallas as pl
from jax.experimental.pallas import tpu as pltpu
from jax.sharding import PartitionSpec as P

HD = 128
SEQ = 128
MESH = pl.DeviceIdType.MESH
NT = (((1,), (1,)), ((), ()))
TN = (((0,), (0,)), ((), ()))
BF16 = jnp.bfloat16
F32 = jnp.float32
COPIES = 128
SLOT = {1: 1, 3: 2, 2: 3}


def rope_tables():
    positions = np.arange(SEQ).astype(np.float32)
    inverse = np.exp(
        -(np.float32(2.0) * np.arange(HD // 2).astype(np.float32) / np.float32(HD))
        * np.float32(math.log(10000.0))
    )
    angles = positions[:, None] * inverse[None, :].astype(np.float32)
    cosine = np.cos(angles).astype(np.float32)
    sine = np.sin(angles).astype(np.float32)
    return (
        np.concatenate([cosine, cosine], axis=1),
        np.concatenate([-sine, sine], axis=1),
    )


def kernel(
    x_hbm, w_hbm, q_hbm, k_hbm, v_hbm, g_hbm, doc_hbm, cos_hbm, sin_hbm,
    ig_ref, wg_ref,
    keep_ref, q_ref, k_ref, v_ref, g_ref, doc_ref, cos_ref, sin_ref,
    w_buf, x_buf, g_buf, g_tok, p_buf, p_sib, z_out, z_one, z_two,
    t_buf, r_one, r_two, m_out, m_in,
    l_sem, send_sem, recv_sem,
):
    t = lax.axis_index("tensor")
    m = lax.axis_index("mirror")
    d = lax.axis_index("dp")
    zh, c = lax.div(t, 2), lax.rem(t, 2)
    x, y = lax.div(d, 4), lax.rem(d, 4)

    def at_z(step):
        return {"tensor": lax.rem(zh + step, 4) * 2 + c}

    def at_x(step):
        return {"dp": lax.rem(x + step, 4) * 4 + y}

    def at_y(step):
        return {"dp": x * 4 + lax.rem(y + step, 4)}

    sibling = {"tensor": zh * 2 + 1 - c}
    twin = {"mirror": 1 - m}

    barrier = pltpu.get_barrier_semaphore()
    partners = [sibling, at_z(1), at_z(3), at_x(1), at_x(2), at_x(3), at_y(1), at_y(3), twin]
    for partner in partners:
        pl.semaphore_signal(barrier, inc=1, device_id=partner, device_id_type=MESH)

    def load(src, dst, index):
        copy = pltpu.make_async_copy(src, dst, l_sem.at[index])
        copy.start()
        return copy

    ready = [
        load(q_hbm.at[0], q_ref, 0),
        load(k_hbm.at[0], k_ref, 1),
        load(cos_hbm, cos_ref, 2),
        load(sin_hbm, sin_ref, 3),
        load(g_hbm.at[0], g_ref, 4),
        load(v_hbm.at[0], v_ref, 5),
        load(doc_hbm, doc_ref, 6),
    ]
    halves = (1 - m, m)
    own_in = [
        load(
            x_hbm.at[0, :, pl.ds(pl.multiple_of(halves[u] * 2048 + x * 512, 512), 512)],
            x_buf.at[u, 0, pl.ds(pl.multiple_of(t * 32, 32), 32)],
            7 + u,
        )
        for u in range(2)
    ]
    w_in = []
    def load_finish():
        for copy in ready:
            copy.wait()
        row = lax.broadcasted_iota(jnp.int32, (SEQ, SEQ), 0)
        col = lax.broadcasted_iota(jnp.int32, (SEQ, SEQ), 1)
        for s in range(2):
            docs = jnp.broadcast_to(doc_ref[:, s * SEQ : (s + 1) * SEQ].astype(F32), (SEQ, SEQ))
            keep_ref[s] = jnp.where((col <= row) & (docs == docs.T), 1.0, 0.0)

    def w_start():
        for i in range(8):
            w_in.append(load(w_hbm.at[pl.ds(i * 512, 512)], w_buf.at[i], 9 + i))

    def half(pair, j, s):
        head(pair, j, (s,))

    def meet():
        pl.semaphore_wait(barrier, len(partners))

    sent = []

    def send(src, dst, device):
        index = len(sent)
        copy = pltpu.make_async_remote_copy(
            src_ref=src,
            dst_ref=dst,
            send_sem=send_sem.at[index],
            recv_sem=recv_sem.at[index],
            device_id=device,
            device_id_type=MESH,
        )
        copy.start()
        sent.append(copy)
        return copy

    turned = {}

    def turn(u):
        turned[u] = []
        for step in (1, 3, 2):
            column = pl.multiple_of(halves[u] * 2048 + lax.rem(x + step, 4) * 512, 512)
            turned[u].append(
                send(
                    x_hbm.at[0, :, pl.ds(column, 512)],
                    x_buf.at[u, SLOT[step], pl.ds(pl.multiple_of(t * 32, 32), 32)],
                    at_x(step),
                )
            )

    def turn_near(u):
        turned[u][0].wait_recv()
        turned[u][1].wait_recv()

    def turn_far(u):
        turned[u][2].wait_recv()

    def own_finish():
        for copy in own_in:
            copy.wait()

    def piece(which, zi, half=None):
        start = (lax.rem(zi, 4) * 2 + c) * 32
        if half is None:
            rows = pl.ds(pl.multiple_of(start, 32), 32)
        else:
            rows = pl.ds(pl.multiple_of(start + 16 * half, 16), 16)
        return (
            x_buf.at[:, 0, rows],
            x_buf.at[0, pl.ds(1, 2), rows],
            x_buf.at[0, 3, rows],
            x_buf.at[1, pl.ds(1, 3), rows],
        )[which]

    ring = {}

    def x_start(which):
        own = piece(which, zh)
        ring[which] = [send(own, own, at_z(1)), send(own, own, at_z(3))]
        ring[which, "sib"] = [send(own, own, sibling)]

    def x_forward(which):
        up, down = ring[which]
        up.wait_recv()
        half = piece(which, zh + 3, 0)
        fu = send(half, half, at_z(1))
        whole = piece(which, zh + 3)
        s_up = send(whole, whole, sibling)
        down.wait_recv()
        half = piece(which, zh + 1, 1)
        fd = send(half, half, at_z(3))
        whole = piece(which, zh + 1)
        s_down = send(whole, whole, sibling)
        ring[which, "far"] = [fu, fd]
        ring[which, "sib"] += [s_up, s_down]

    def x_far(which):
        fu, fd = ring[which, "far"]
        fu.wait_recv()
        half = piece(which, zh + 2, 0)
        s_up = send(half, half, sibling)
        fd.wait_recv()
        half = piece(which, zh + 2, 1)
        s_down = send(half, half, sibling)
        ring[which, "sib"] += [s_up, s_down]

    def x_finish(which):
        for copy in ring[which, "sib"]:
            copy.wait_recv()

    scale = 1.0 / math.sqrt(HD)

    def rotate(values):
        return values * cos_ref[...] + pltpu.roll(values, 64, 1) * sin_ref[...]

    def unrotate(values):
        return values * cos_ref[...] - pltpu.roll(values, 64, 1) * sin_ref[...]

    def head(pair, j, sequences=(0, 1)):
        h = 2 * pair + j
        for s in sequences:
            rows = slice(s * SEQ, (s + 1) * SEQ)
            cols = slice(h * HD, (h + 1) * HD)
            q_rot = rotate(q_ref[rows, cols].astype(F32)).astype(BF16)
            k_rot = rotate(k_ref[rows, cols].astype(F32)).astype(BF16)
            scores = lax.dot_general(q_rot, k_rot, NT, preferred_element_type=F32) * scale
            scores = jnp.where(keep_ref[s] > 0.5, scores, -1e30)
            exps = jnp.exp(scores - jnp.max(scores, axis=-1, keepdims=True))
            probs = exps / jnp.sum(exps, axis=-1, keepdims=True)
            dprob = lax.dot_general(
                g_ref[rows, cols], v_ref[rows, cols], NT, preferred_element_type=F32
            )
            delta = jnp.sum(probs * dprob, axis=-1, keepdims=True)
            dscore = (probs * (dprob - delta)).astype(BF16)
            dq = jnp.dot(dscore, k_rot, preferred_element_type=F32) * scale
            dk = lax.dot_general(dscore, q_rot, TN, preferred_element_type=F32) * scale
            dq, dk = unrotate(dq), unrotate(dk)
            g_tok[rows, h * HD : (h + 1) * HD] = dq.astype(BF16)
            g_tok[rows, 512 + h * HD : 512 + (h + 1) * HD] = dk.astype(BF16)
            g_buf[pair, j * 256 : j * 256 + 128, rows] = dq.T.astype(BF16)
            g_buf[pair, j * 256 + 128 : j * 256 + 256, rows] = dk.T.astype(BF16)

    grads = {}

    def g_part(h, slot, half=0):
        first, size = ((0, 256), (0, 96), (96, 160))[half]
        row = (h % 2) * 256 + first
        return g_buf.at[h // 2, pl.ds(row, size), pl.ds(slot * 256, 256)]

    def g_start(h):
        grads[h] = [
            send(g_part(h, 0), g_part(h, 1), at_x(1)),
            send(g_part(h, 0), g_part(h, 2), at_x(3)),
        ]

    def g_forward(h):
        up, down = grads[h]
        up.wait_recv()
        fu = send(g_part(h, 1, 1), g_part(h, 3, 1), at_x(1))
        down.wait_recv()
        fd = send(g_part(h, 2, 2), g_part(h, 3, 2), at_x(3))
        grads[h, "far"] = [fu, fd]

    def g_finish(h):
        for copy in grads[h, "far"]:
            copy.wait_recv()

    pick_row = lax.broadcasted_iota(jnp.int32, (256, 256), 0)
    pick_col = lax.broadcasted_iota(jnp.int32, (256, 256), 1)
    pick = jnp.where(
        pick_col == jnp.where(pick_row < 128, 2 * pick_row, 2 * pick_row - 255), 1.0, 0.0
    ).astype(BF16)
    swaps = {}

    def p_half(i):
        u, off = i // 2, (i % 2) * 512
        w_in[i].wait()
        mixed = w_buf[i].reshape(1024, 512)
        parts = [
            jnp.dot(pick, mixed[b * 256 : (b + 1) * 256], preferred_element_type=F32).astype(BF16)
            for b in range(4)
        ]
        w_q = jnp.concatenate([part[:128] for part in parts], axis=0)
        w_k = jnp.concatenate([part[128:] for part in parts], axis=0)
        partial = lax.dot_general(
            g_tok[:, :512], w_q, NT, preferred_element_type=F32
        ) + lax.dot_general(g_tok[:, 512:], w_k, NT, preferred_element_type=F32)
        p_buf[u, :, :, :, off : off + 512] = partial.astype(BF16).reshape(4, 2, 32, 512)
        if i % 2:
            swaps[u] = send(p_buf.at[u, :, 1 - c], p_sib.at[u], sibling)

    def p_sum(u, zi):
        return p_buf[u, zi, c].astype(F32) + p_sib[u, zi].astype(F32)

    def p_one(u):
        swaps[u].wait_recv()
        z_out[u, 0] = p_sum(u, lax.rem(zh + 2, 4)).astype(BF16)
        low, high = pl.ds(0, 16), pl.ds(16, 16)
        swaps[u, 1] = [
            send(z_out.at[u, 0, low], z_one.at[u, 0], at_z(1)),
            send(z_out.at[u, 0, high], z_one.at[u, 1], at_z(3)),
        ]

    def p_two(u):
        up, down = swaps[u, 1]
        up.wait_recv()
        total = p_sum(u, lax.rem(zh + 1, 4))
        z_out[u, 1, :16] = (total[:16] + z_one[u, 0].astype(F32)).astype(BF16)
        z_out[u, 1, 16:] = total[16:].astype(BF16)
        fu = send(z_out.at[u, 1], z_two.at[u, 0], at_z(1))
        down.wait_recv()
        total = p_sum(u, lax.rem(zh + 3, 4))
        z_out[u, 2, :16] = total[:16].astype(BF16)
        z_out[u, 2, 16:] = (total[16:] + z_one[u, 1].astype(F32)).astype(BF16)
        fd = send(z_out.at[u, 2], z_two.at[u, 1], at_z(3))
        swaps[u, 2] = [fu, fd]

    def p_end(u):
        for copy in swaps[u, 2]:
            copy.wait_recv()
        total = p_sum(u, zh) + z_two[u, 0].astype(F32) + z_two[u, 1].astype(F32)
        ig_ref[:, u * 1024 : (u + 1) * 1024] = total.astype(BF16)

    terms = {}

    def t_unit(u, h):
        left = g_buf[h // 2, (h % 2) * 256 : (h % 2) * 256 + 256]
        term = jnp.dot(left, x_buf[u].reshape(1024, 512), preferred_element_type=F32)
        for b in range(4):
            t_buf[u, h, b] = term[:, b * 128 : (b + 1) * 128].astype(BF16)
        far = lax.rem(y + 2, 4)
        n = 4 * u + h
        terms[n] = [
            send(t_buf.at[u, h, far, pl.ds(0, 128)], r_one.at[n, 0], at_y(1)),
            send(t_buf.at[u, h, far, pl.ds(128, 128)], r_one.at[n, 1], at_y(3)),
        ]

    def t_two(u, h):
        n = 4 * u + h
        up, down = terms[n]
        up.wait_recv()
        b = lax.rem(y + 1, 4)
        t_buf[u, h, b, :128] = (
            t_buf[u, h, b, :128].astype(F32) + r_one[n, 0].astype(F32)
        ).astype(BF16)
        fu = send(t_buf.at[u, h, b], r_two.at[n, 0], at_y(1))
        down.wait_recv()
        b = lax.rem(y + 3, 4)
        t_buf[u, h, b, 128:] = (
            t_buf[u, h, b, 128:].astype(F32) + r_one[n, 1].astype(F32)
        ).astype(BF16)
        fd = send(t_buf.at[u, h, b], r_two.at[n, 1], at_y(3))
        terms[n, 2] = [fu, fd]

    def t_sum(u, h):
        n = 4 * u + h
        for copy in terms[n, 2]:
            copy.wait_recv()
        return t_buf[u, h, y].astype(F32) + r_two[n, 0].astype(F32) + r_two[n, 1].astype(F32)

    def t_away(h):
        m_out[h] = t_sum(0, h).astype(BF16)
        terms["m", h] = send(m_out.at[h], m_in.at[h], twin)

    def t_end(h):
        total = t_sum(1, h)
        terms["m", h].wait_recv()
        total = (total + m_in[h].astype(F32)) * (1.0 / 32.0)
        for p in range(2):
            wg_ref[:, p, h * 128 : h * 128 + 128] = total[p * 128 : p * 128 + 128].T

    load_finish()
    w_start()
    own_finish()
    meet()
    x_start(0)
    turn(0)
    turn(1)
    half(0, 0, 0)
    half(0, 0, 1)
    head(0, 1)
    g_start(0)
    head(1, 0)
    turn_near(0)
    x_start(1)
    g_start(1)
    head(1, 1)
    g_start(2)
    g_start(3)
    p_half(0)
    turn_far(0)
    x_start(2)
    p_half(1)
    turn_far(1)
    turn_near(1)
    x_start(3)
    p_half(2)
    p_half(3)
    p_half(4)
    x_forward(2)
    g_forward(0)
    x_forward(0)
    p_half(5)
    x_forward(1)
    g_forward(1)
    p_half(6)
    p_half(7)
    p_one(0)
    g_forward(2)
    x_forward(3)
    p_one(3)
    p_one(1)
    x_far(2)
    g_forward(3)
    x_far(0)
    x_far(1)
    x_finish(2)
    g_finish(0)
    p_one(2)
    x_finish(0)
    x_finish(1)
    t_unit(0, 0)
    p_two(0)
    g_finish(1)
    t_unit(0, 1)
    g_finish(3)
    g_finish(2)
    t_unit(0, 2)
    t_unit(0, 3)
    x_far(3)
    t_two(0, 0)
    p_two(1)
    x_finish(3)
    t_unit(1, 1)
    t_unit(1, 2)
    t_unit(1, 0)
    p_two(3)
    t_two(0, 2)
    p_two(2)
    t_two(0, 3)
    t_unit(1, 3)
    t_two(0, 1)
    t_away(0)
    t_two(1, 2)
    t_away(2)
    t_two(1, 1)
    t_two(1, 0)
    t_away(3)
    t_two(1, 3)
    t_away(1)
    p_end(1)
    t_end(0)
    p_end(2)
    p_end(3)
    t_end(2)
    p_end(0)
    t_end(3)
    t_end(1)
    for copy in sent:
        copy.wait_send()


def hand_over(ig_in, wg_in, ig_out, wg_out, sem):
    copies = [
        pltpu.make_async_copy(wg_in, wg_out, sem.at[0]),
        pltpu.make_async_copy(ig_in, ig_out.at[0], sem.at[1]),
    ]
    for copy in copies:
        copy.start()
    for copy in copies:
        copy.wait()


def shards(layer_input, qk_weight, query_proj, key_proj, value_proj, head_grad, doc_ids):
    cosine, sine = rope_tables()
    hbm = pl.BlockSpec(memory_space=pl.ANY)
    vmem = pl.BlockSpec(memory_space=pltpu.VMEM)
    dma = pltpu.SemaphoreType.DMA
    input_grad, weight_grad = pl.pallas_call(
        kernel,
        out_shape=(
            pltpu.VMEM((32, 4096), BF16),
            pltpu.VMEM((128, 2, 512), F32),
        ),
        in_specs=[hbm] * 9,
        out_specs=(vmem, vmem),
        scratch_shapes=[
            pltpu.VMEM((2, 128, 128), F32),
            pltpu.VMEM((256, 512), BF16),
            pltpu.VMEM((256, 512), BF16),
            pltpu.VMEM((256, 512), BF16),
            pltpu.VMEM((256, 512), BF16),
            pltpu.VMEM((1, 256), jnp.int32),
            pltpu.VMEM((128, 128), F32),
            pltpu.VMEM((128, 128), F32),
            pltpu.VMEM((8, 512, 2, 512), BF16),
            pltpu.VMEM((2, 4, 256, 512), BF16),
            pltpu.VMEM((2, 512, 1024), BF16),
            pltpu.VMEM((256, 1024), BF16),
            pltpu.VMEM((4, 4, 2, 32, 1024), BF16),
            pltpu.VMEM((4, 4, 32, 1024), BF16),
            pltpu.VMEM((4, 3, 32, 1024), BF16),
            pltpu.VMEM((4, 2, 16, 1024), BF16),
            pltpu.VMEM((4, 2, 32, 1024), BF16),
            pltpu.VMEM((2, 4, 4, 256, 128), BF16),
            pltpu.VMEM((8, 2, 128, 128), BF16),
            pltpu.VMEM((8, 2, 256, 128), BF16),
            pltpu.VMEM((4, 256, 128), BF16),
            pltpu.VMEM((4, 256, 128), BF16),
            dma((17,)),
            dma((COPIES,)),
            dma((COPIES,)),
        ],
        compiler_params=pltpu.CompilerParams(
            collective_id=0, has_side_effects=True, vmem_limit_bytes=58 << 20
        ),
        name="qk_backward",
    )(
        layer_input, qk_weight, query_proj, key_proj, value_proj, head_grad, doc_ids,
        jnp.asarray(cosine), jnp.asarray(sine),
    )
    return pl.pallas_call(
        hand_over,
        out_shape=(
            jax.ShapeDtypeStruct((1, 32, 4096), BF16),
            jax.ShapeDtypeStruct((128, 2, 512), F32),
        ),
        in_specs=[vmem] * 2,
        out_specs=(hbm, hbm),
        scratch_shapes=[dma((2,))],
        compiler_params=pltpu.CompilerParams(vmem_limit_bytes=16 << 20),
        name="hand_over",
    )(input_grad, weight_grad)


def solution(mesh):
    rows = ("mirror", "dp")
    in_specs = (
        P(rows, "tensor", None),
        P(None, None, "tensor"),
        P(rows, None, "tensor"),
        P(rows, None, "tensor"),
        P(rows, None, "tensor"),
        P(rows, None, "tensor"),
        P(rows, None),
    )
    out_specs = (P(rows, "tensor", None), P(rows, None, "tensor"))
    return jax.shard_map(shards, mesh=mesh, in_specs=in_specs, out_specs=out_specs, check_vma=False)
```

```python
import functools
import math

import jax
import jax.numpy as jnp
import numpy as np
from jax import lax
from jax.experimental import pallas as pl
from jax.experimental.pallas import tpu as pltpu
from jax.sharding import PartitionSpec as P

HD = 128
SEQ = 128
MESH = pl.DeviceIdType.MESH
NT = (((1,), (1,)), ((), ()))
TN = (((0,), (0,)), ((), ()))
BF16 = jnp.bfloat16
F32 = jnp.float32
COPIES = 128
SLOT = {1: 1, 3: 2, 2: 3}


def rope_tables():
    positions = np.arange(SEQ).astype(np.float32)
    inverse = np.exp(
        -(np.float32(2.0) * np.arange(HD // 2).astype(np.float32) / np.float32(HD))
        * np.float32(math.log(10000.0))
    )
    angles = positions[:, None] * inverse[None, :].astype(np.float32)
    cosine = np.cos(angles).astype(np.float32)
    sine = np.sin(angles).astype(np.float32)
    return (
        np.concatenate([cosine, cosine], axis=1),
        np.concatenate([-sine, sine], axis=1),
    )


def kernel(
    x_hbm, w_hbm, q_hbm, k_hbm, v_hbm, g_hbm, doc_hbm, cos_hbm, sin_hbm,
    ig_ref, wg_ref,
    keep_ref, q_ref, k_ref, v_ref, g_ref, doc_ref, cos_ref, sin_ref,
    w_buf, x_buf, g_buf, g_tok, p_buf, p_sib, z_out, z_one, z_two,
    t_buf, r_one, r_two, m_out, m_in,
    l_sem, send_sem, recv_sem,
):
    t = lax.axis_index("tensor")
    m = lax.axis_index("mirror")
    d = lax.axis_index("dp")
    zh, c = lax.div(t, 2), lax.rem(t, 2)
    x, y = lax.div(d, 4), lax.rem(d, 4)

    def at_z(step):
        return {"tensor": lax.rem(zh + step, 4) * 2 + c}

    def at_x(step):
        return {"dp": lax.rem(x + step, 4) * 4 + y}

    def at_y(step):
        return {"dp": x * 4 + lax.rem(y + step, 4)}

    sibling = {"tensor": zh * 2 + 1 - c}
    twin = {"mirror": 1 - m}

    barrier = pltpu.get_barrier_semaphore()
    partners = [sibling, at_z(1), at_z(3), at_x(1), at_x(2), at_x(3), at_y(1), at_y(3), twin]
    for partner in partners:
        pl.semaphore_signal(barrier, inc=1, device_id=partner, device_id_type=MESH)

    def load(src, dst, index):
        copy = pltpu.make_async_copy(src, dst, l_sem.at[index])
        copy.start()
        return copy

    ready = [
        load(q_hbm.at[0], q_ref, 0),
        load(k_hbm.at[0], k_ref, 1),
        load(cos_hbm, cos_ref, 2),
        load(sin_hbm, sin_ref, 3),
        load(g_hbm.at[0], g_ref, 4),
        load(v_hbm.at[0], v_ref, 5),
        load(doc_hbm, doc_ref, 6),
    ]
    halves = (1 - m, m)
    own_in = [
        load(
            x_hbm.at[0, :, pl.ds(pl.multiple_of(halves[u] * 2048 + x * 512, 512), 512)],
            x_buf.at[u, 0, pl.ds(pl.multiple_of(t * 32, 32), 32)],
            7 + u,
        )
        for u in range(2)
    ]
    w_in = []
    def load_finish():
        for copy in ready:
            copy.wait()
        row = lax.broadcasted_iota(jnp.int32, (SEQ, SEQ), 0)
        col = lax.broadcasted_iota(jnp.int32, (SEQ, SEQ), 1)
        for s in range(2):
            docs = jnp.broadcast_to(doc_ref[:, s * SEQ : (s + 1) * SEQ].astype(F32), (SEQ, SEQ))
            keep_ref[s] = jnp.where((col <= row) & (docs == docs.T), 1.0, 0.0)

    def w_start():
        for i in range(8):
            w_in.append(load(w_hbm.at[pl.ds(i * 512, 512)], w_buf.at[i], 9 + i))

    def half(pair, j, s):
        head(pair, j, (s,))

    def meet():
        pl.semaphore_wait(barrier, len(partners))

    sent = []

    def send(src, dst, device):
        index = len(sent)
        copy = pltpu.make_async_remote_copy(
            src_ref=src,
            dst_ref=dst,
            send_sem=send_sem.at[index],
            recv_sem=recv_sem.at[index],
            device_id=device,
            device_id_type=MESH,
        )
        copy.start()
        sent.append(copy)
        return copy

    turned = {}

    def turn(u):
        turned[u] = []
        for step in (1, 3, 2):
            column = pl.multiple_of(halves[u] * 2048 + lax.rem(x + step, 4) * 512, 512)
            turned[u].append(
                send(
                    x_hbm.at[0, :, pl.ds(column, 512)],
                    x_buf.at[u, SLOT[step], pl.ds(pl.multiple_of(t * 32, 32), 32)],
                    at_x(step),
                )
            )

    def turn_near(u):
        turned[u][0].wait_recv()
        turned[u][1].wait_recv()

    def turn_far(u):
        turned[u][2].wait_recv()

    def own_finish():
        for copy in own_in:
            copy.wait()

    def piece(which, zi, half=None):
        start = (lax.rem(zi, 4) * 2 + c) * 32
        if half is None:
            rows = pl.ds(pl.multiple_of(start, 32), 32)
        else:
            rows = pl.ds(pl.multiple_of(start + 16 * half, 16), 16)
        return (
            x_buf.at[:, 0, rows],
            x_buf.at[0, pl.ds(1, 2), rows],
            x_buf.at[0, 3, rows],
            x_buf.at[1, pl.ds(1, 3), rows],
        )[which]

    ring = {}

    def x_start(which):
        own = piece(which, zh)
        ring[which] = [send(own, own, at_z(1)), send(own, own, at_z(3))]
        ring[which, "sib"] = [send(own, own, sibling)]

    def x_forward(which):
        up, down = ring[which]
        up.wait_recv()
        half = piece(which, zh + 3, 0)
        fu = send(half, half, at_z(1))
        whole = piece(which, zh + 3)
        s_up = send(whole, whole, sibling)
        down.wait_recv()
        half = piece(which, zh + 1, 1)
        fd = send(half, half, at_z(3))
        whole = piece(which, zh + 1)
        s_down = send(whole, whole, sibling)
        ring[which, "far"] = [fu, fd]
        ring[which, "sib"] += [s_up, s_down]

    def x_far(which):
        fu, fd = ring[which, "far"]
        fu.wait_recv()
        half = piece(which, zh + 2, 0)
        s_up = send(half, half, sibling)
        fd.wait_recv()
        half = piece(which, zh + 2, 1)
        s_down = send(half, half, sibling)
        ring[which, "sib"] += [s_up, s_down]

    def x_finish(which):
        for copy in ring[which, "sib"]:
            copy.wait_recv()

    scale = 1.0 / math.sqrt(HD)

    def rotate(values):
        return values * cos_ref[...] + pltpu.roll(values, 64, 1) * sin_ref[...]

    def unrotate(values):
        return values * cos_ref[...] - pltpu.roll(values, 64, 1) * sin_ref[...]

    def head(pair, j, sequences=(0, 1)):
        h = 2 * pair + j
        for s in sequences:
            rows = slice(s * SEQ, (s + 1) * SEQ)
            cols = slice(h * HD, (h + 1) * HD)
            q_rot = rotate(q_ref[rows, cols].astype(F32)).astype(BF16)
            k_rot = rotate(k_ref[rows, cols].astype(F32)).astype(BF16)
            scores = lax.dot_general(q_rot, k_rot, NT, preferred_element_type=F32) * scale
            scores = jnp.where(keep_ref[s] > 0.5, scores, -1e30)
            exps = jnp.exp(scores - jnp.max(scores, axis=-1, keepdims=True))
            probs = exps / jnp.sum(exps, axis=-1, keepdims=True)
            dprob = lax.dot_general(
                g_ref[rows, cols], v_ref[rows, cols], NT, preferred_element_type=F32
            )
            delta = jnp.sum(probs * dprob, axis=-1, keepdims=True)
            dscore = (probs * (dprob - delta)).astype(BF16)
            dq = jnp.dot(dscore, k_rot, preferred_element_type=F32) * scale
            dk = lax.dot_general(dscore, q_rot, TN, preferred_element_type=F32) * scale
            dq, dk = unrotate(dq), unrotate(dk)
            g_tok[rows, h * HD : (h + 1) * HD] = dq.astype(BF16)
            g_tok[rows, 512 + h * HD : 512 + (h + 1) * HD] = dk.astype(BF16)
            g_buf[pair, j * 256 : j * 256 + 128, rows] = dq.T.astype(BF16)
            g_buf[pair, j * 256 + 128 : j * 256 + 256, rows] = dk.T.astype(BF16)

    grads = {}

    def g_part(h, slot, half=0):
        first, size = ((0, 256), (0, 96), (96, 160))[half]
        row = (h % 2) * 256 + first
        return g_buf.at[h // 2, pl.ds(row, size), pl.ds(slot * 256, 256)]

    def g_start(h):
        grads[h] = [
            send(g_part(h, 0), g_part(h, 1), at_x(1)),
            send(g_part(h, 0), g_part(h, 2), at_x(3)),
        ]

    def g_forward(h):
        up, down = grads[h]
        up.wait_recv()
        fu = send(g_part(h, 1, 1), g_part(h, 3, 1), at_x(1))
        down.wait_recv()
        fd = send(g_part(h, 2, 2), g_part(h, 3, 2), at_x(3))
        grads[h, "far"] = [fu, fd]

    def g_finish(h):
        for copy in grads[h, "far"]:
            copy.wait_recv()

    pick_row = lax.broadcasted_iota(jnp.int32, (256, 256), 0)
    pick_col = lax.broadcasted_iota(jnp.int32, (256, 256), 1)
    pick = jnp.where(
        pick_col == jnp.where(pick_row < 128, 2 * pick_row, 2 * pick_row - 255), 1.0, 0.0
    ).astype(BF16)
    swaps = {}

    def p_half(i):
        u, off = i // 2, (i % 2) * 512
        w_in[i].wait()
        mixed = w_buf[i].reshape(1024, 512)
        parts = [
            jnp.dot(pick, mixed[b * 256 : (b + 1) * 256], preferred_element_type=F32).astype(BF16)
            for b in range(4)
        ]
        w_q = jnp.concatenate([part[:128] for part in parts], axis=0)
        w_k = jnp.concatenate([part[128:] for part in parts], axis=0)
        partial = lax.dot_general(
            g_tok[:, :512], w_q, NT, preferred_element_type=F32
        ) + lax.dot_general(g_tok[:, 512:], w_k, NT, preferred_element_type=F32)
        p_buf[u, :, :, :, off : off + 512] = partial.astype(BF16).reshape(4, 2, 32, 512)
        if i % 2:
            swaps[u] = send(p_buf.at[u, :, 1 - c], p_sib.at[u], sibling)

    def p_sum(u, zi):
        return p_buf[u, zi, c].astype(F32) + p_sib[u, zi].astype(F32)

    def p_one(u):
        swaps[u].wait_recv()
        z_out[u, 0] = p_sum(u, lax.rem(zh + 2, 4)).astype(BF16)
        low, high = pl.ds(0, 16), pl.ds(16, 16)
        swaps[u, 1] = [
            send(z_out.at[u, 0, low], z_one.at[u, 0], at_z(1)),
            send(z_out.at[u, 0, high], z_one.at[u, 1], at_z(3)),
        ]

    def p_two(u):
        up, down = swaps[u, 1]
        up.wait_recv()
        total = p_sum(u, lax.rem(zh + 1, 4))
        z_out[u, 1, :16] = (total[:16] + z_one[u, 0].astype(F32)).astype(BF16)
        z_out[u, 1, 16:] = total[16:].astype(BF16)
        fu = send(z_out.at[u, 1], z_two.at[u, 0], at_z(1))
        down.wait_recv()
        total = p_sum(u, lax.rem(zh + 3, 4))
        z_out[u, 2, :16] = total[:16].astype(BF16)
        z_out[u, 2, 16:] = (total[16:] + z_one[u, 1].astype(F32)).astype(BF16)
        fd = send(z_out.at[u, 2], z_two.at[u, 1], at_z(3))
        swaps[u, 2] = [fu, fd]

    def p_end(u):
        for copy in swaps[u, 2]:
            copy.wait_recv()
        total = p_sum(u, zh) + z_two[u, 0].astype(F32) + z_two[u, 1].astype(F32)
        ig_ref[:, u * 1024 : (u + 1) * 1024] = total.astype(BF16)

    terms = {}

    def t_unit(u, h):
        left = g_buf[h // 2, (h % 2) * 256 : (h % 2) * 256 + 256]
        term = jnp.dot(left, x_buf[u].reshape(1024, 512), preferred_element_type=F32)
        for b in range(4):
            t_buf[u, h, b] = term[:, b * 128 : (b + 1) * 128].astype(BF16)
        far = lax.rem(y + 2, 4)
        n = 4 * u + h
        terms[n] = [
            send(t_buf.at[u, h, far, pl.ds(0, 128)], r_one.at[n, 0], at_y(1)),
            send(t_buf.at[u, h, far, pl.ds(128, 128)], r_one.at[n, 1], at_y(3)),
        ]

    def t_two(u, h):
        n = 4 * u + h
        up, down = terms[n]
        up.wait_recv()
        b = lax.rem(y + 1, 4)
        t_buf[u, h, b, :128] = (
            t_buf[u, h, b, :128].astype(F32) + r_one[n, 0].astype(F32)
        ).astype(BF16)
        fu = send(t_buf.at[u, h, b], r_two.at[n, 0], at_y(1))
        down.wait_recv()
        b = lax.rem(y + 3, 4)
        t_buf[u, h, b, 128:] = (
            t_buf[u, h, b, 128:].astype(F32) + r_one[n, 1].astype(F32)
        ).astype(BF16)
        fd = send(t_buf.at[u, h, b], r_two.at[n, 1], at_y(3))
        terms[n, 2] = [fu, fd]

    def t_sum(u, h):
        n = 4 * u + h
        for copy in terms[n, 2]:
            copy.wait_recv()
        return t_buf[u, h, y].astype(F32) + r_two[n, 0].astype(F32) + r_two[n, 1].astype(F32)

    def t_away(h):
        m_out[h] = t_sum(0, h).astype(BF16)
        terms["m", h] = send(m_out.at[h], m_in.at[h], twin)

    def t_end(h):
        total = t_sum(1, h)
        terms["m", h].wait_recv()
        total = (total + m_in[h].astype(F32)) * (1.0 / 32.0)
        for p in range(2):
            wg_ref[:, p, h * 128 : h * 128 + 128] = total[p * 128 : p * 128 + 128].T

    load_finish()
    w_start()
    own_finish()
    meet()
    x_start(0)
    turn(0)
    turn(1)
    half(0, 0, 0)
    half(0, 0, 1)
    head(0, 1)
    g_start(0)
    head(1, 0)
    turn_near(0)
    x_start(1)
    g_start(1)
    head(1, 1)
    g_start(2)
    g_start(3)
    p_half(0)
    turn_far(0)
    x_start(2)
    p_half(1)
    turn_far(1)
    turn_near(1)
    x_start(3)
    p_half(2)
    p_half(3)
    p_half(4)
    x_forward(2)
    g_forward(0)
    x_forward(0)
    p_half(5)
    x_forward(1)
    g_forward(1)
    p_half(6)
    p_half(7)
    p_one(0)
    g_forward(2)
    x_forward(3)
    p_one(3)
    p_one(1)
    x_far(2)
    g_forward(3)
    x_far(0)
    x_far(1)
    x_finish(2)
    g_finish(0)
    p_one(2)
    x_finish(0)
    x_finish(1)
    t_unit(0, 0)
    p_two(0)
    g_finish(1)
    t_unit(0, 1)
    g_finish(3)
    g_finish(2)
    t_unit(0, 2)
    t_unit(0, 3)
    x_far(3)
    t_two(0, 0)
    p_two(1)
    x_finish(3)
    t_unit(1, 1)
    t_unit(1, 2)
    t_unit(1, 0)
    p_two(3)
    t_two(0, 2)
    p_two(2)
    t_two(0, 3)
    t_unit(1, 3)
    t_two(0, 1)
    t_away(0)
    t_two(1, 2)
    t_away(2)
    t_two(1, 1)
    t_two(1, 0)
    t_away(3)
    t_two(1, 3)
    t_away(1)
    p_end(1)
    t_end(0)
    p_end(2)
    p_end(3)
    t_end(2)
    p_end(0)
    t_end(3)
    t_end(1)
    for copy in sent:
        copy.wait_send()


def hand_over(ig_in, wg_in, ig_out, wg_out, sem):
    copies = []
    for i in range(4):
        rows = pl.ds(32 * i, 32)
        copies.append(pltpu.make_async_copy(wg_in.at[rows], wg_out.at[rows], sem.at[i]))
    for i in range(2):
        rows = pl.ds(16 * i, 16)
        copies.append(pltpu.make_async_copy(ig_in.at[rows], ig_out.at[0, rows], sem.at[4 + i]))
    for copy in copies:
        copy.start()
    for copy in copies:
        copy.wait()


def shards(layer_input, qk_weight, query_proj, key_proj, value_proj, head_grad, doc_ids):
    cosine, sine = rope_tables()
    hbm = pl.BlockSpec(memory_space=pl.ANY)
    vmem = pl.BlockSpec(memory_space=pltpu.VMEM)
    dma = pltpu.SemaphoreType.DMA
    input_grad, weight_grad = pl.pallas_call(
        kernel,
        out_shape=(
            pltpu.VMEM((32, 4096), BF16),
            pltpu.VMEM((128, 2, 512), F32),
        ),
        in_specs=[hbm] * 9,
        out_specs=(vmem, vmem),
        scratch_shapes=[
            pltpu.VMEM((2, 128, 128), F32),
            pltpu.VMEM((256, 512), BF16),
            pltpu.VMEM((256, 512), BF16),
            pltpu.VMEM((256, 512), BF16),
            pltpu.VMEM((256, 512), BF16),
            pltpu.VMEM((1, 256), jnp.int32),
            pltpu.VMEM((128, 128), F32),
            pltpu.VMEM((128, 128), F32),
            pltpu.VMEM((8, 512, 2, 512), BF16),
            pltpu.VMEM((2, 4, 256, 512), BF16),
            pltpu.VMEM((2, 512, 1024), BF16),
            pltpu.VMEM((256, 1024), BF16),
            pltpu.VMEM((4, 4, 2, 32, 1024), BF16),
            pltpu.VMEM((4, 4, 32, 1024), BF16),
            pltpu.VMEM((4, 3, 32, 1024), BF16),
            pltpu.VMEM((4, 2, 16, 1024), BF16),
            pltpu.VMEM((4, 2, 32, 1024), BF16),
            pltpu.VMEM((2, 4, 4, 256, 128), BF16),
            pltpu.VMEM((8, 2, 128, 128), BF16),
            pltpu.VMEM((8, 2, 256, 128), BF16),
            pltpu.VMEM((4, 256, 128), BF16),
            pltpu.VMEM((4, 256, 128), BF16),
            dma((17,)),
            dma((COPIES,)),
            dma((COPIES,)),
        ],
        compiler_params=pltpu.CompilerParams(
            collective_id=0, has_side_effects=True, vmem_limit_bytes=58 << 20
        ),
        name="qk_backward",
    )(
        layer_input, qk_weight, query_proj, key_proj, value_proj, head_grad, doc_ids,
        jnp.asarray(cosine), jnp.asarray(sine),
    )
    return pl.pallas_call(
        hand_over,
        out_shape=(
            jax.ShapeDtypeStruct((1, 32, 4096), BF16),
            jax.ShapeDtypeStruct((128, 2, 512), F32),
        ),
        in_specs=[vmem] * 2,
        out_specs=(hbm, hbm),
        scratch_shapes=[dma((6,))],
        compiler_params=pltpu.CompilerParams(vmem_limit_bytes=16 << 20),
        name="hand_over",
    )(input_grad, weight_grad)


def solution(mesh):
    rows = ("mirror", "dp")
    in_specs = (
        P(rows, "tensor", None),
        P(None, None, "tensor"),
        P(rows, None, "tensor"),
        P(rows, None, "tensor"),
        P(rows, None, "tensor"),
        P(rows, None, "tensor"),
        P(rows, None),
    )
    out_specs = (P(rows, "tensor", None), P(rows, None, "tensor"))
    return jax.shard_map(shards, mesh=mesh, in_specs=in_specs, out_specs=out_specs, check_vma=False)
```
